256 devices in a mesh: seq: 128 (over y, x, z), head: 2 (over core).
Axes of the slice: x: 4, y: 4, z: 8, core: 2. Of those that a mesh axis runs over, the one named last changes fastest.
Arguments:
- tokens: bfloat16 [65536, 2048], P('seq', 'head'), may hold values from -6 to 6
- q_weight: bfloat16 [2048, 2048], P(None, 'head'), may hold values from -0.125 to 0.125
- key_matrix: bfloat16 [2048, 512], P(None, 'head'), may hold values from -0.125 to 0.125
- value_matrix: bfloat16 [2048, 512], P(None, 'head'), may hold values from -0.125 to 0.125
- norm_gain: float32 [2048], P('head'), may hold values from 0.1 to 1.9
- out_weight: bfloat16 [2048, 2048], P('head'), may hold values from -0.1875 to 0.1875
- doc_ids: int32 [65536], P('seq'), may hold values from 0 to 63, never falling along the last dimension, each value on 1 to 32768 neighbouring positions
Outputs:
- layer_out: bfloat16 [65536, 2048], P('seq', 'head')
The draws below stay inside these ranges and needn't reach their ends.
Inputs may be any that keep to these rules, and one draw needn't show every extreme that they name: `doc_ids`: document numbers never fall along the window; each of the 64 documents has 1 to 32768 positions, and one has exactly 32768.
All inputs are finite; a program needn't handle non-finite values.
Results may differ from the reference program's by a relative error of at most 0.0095.
Values may be sent and summed in bfloat16 or wider, within the bound.
No kernel may reach another device: no remote copies, remote signals or barrier semaphores. Data moves between devices by JAX's collectives and lax.ppermute only.
A program may use at most 128 MiB of HBM per device.

```python
import math
import jax
import jax.numpy as jnp
import numpy as np
from jax import lax

MODEL_WIDTH = 2048
QUERY_HEADS = 16
KEY_VALUE_HEADS = 4
HEAD_SIZE = 128
TOKENS_PER_SHARD = 512
DOCS = 64
TOKENS = 65536
MOST_DOC = 32768


def with_spikes(drawn, key, source, target, blocks, factor):
    owner, partner = [(jnp.arange(drawn.shape[axis_at]) // (drawn.shape[axis_at] // blocks)).reshape([-1 if axis == axis_at else 1 for axis in range(drawn.ndim)]) for axis_at in (source, target)]
    chosen = jax.random.permutation(key, blocks)[partner]
    strong = (owner == chosen) | (owner == (partner + blocks // 2) % blocks)
    return jnp.where(strong, factor * drawn, drawn)


def steps_of(rng, extent, pieces, smallest, top_value):
    gain, own = 1.0, jax.random.fold_in(rng, 6)
    for axis_at, parts in pieces:
        draws = jnp.exp(jax.random.uniform(jax.random.fold_in(own, axis_at), (parts,), jnp.float32, smallest / len(pieces), top_value / len(pieces)))
        gain = gain * jnp.repeat(draws, extent[axis_at] // parts).reshape([-1 if axis == axis_at else 1 for axis in range(len(extent))])
    return gain


def length_profile(number_of, total, bound, lean):
    weights = [(1 << 20) // math.isqrt(standing ** lean) + 1 for standing in range(2, number_of + 1)]
    spare, given = total - bound - (number_of - 1), [1] * (number_of - 1)
    while spare > 0:
        movable = [i for i in range(number_of - 1) if given[i] < bound]
        pool, left = sum([weights[i] for i in movable]), spare
        for i in movable:
            extra = min(bound - given[i], max(1, left * weights[i] // pool), spare)
            given[i] = given[i] + extra
            spare = spare - extra
    return np.array([bound] + given)


def ragged_sizes(rng, amount, total, bound, skew):
    if amount == 2:
        one = jax.random.randint(rng, (), max(1, total - bound), min(bound, total - 1) + 1)
        return jnp.stack([one, total - one])
    sizes = jnp.asarray(length_profile(amount, total, bound, skew), jnp.int32)
    couples = (amount - 1) // 2
    source_of, taker = sizes[1:1 + 2 * couples:2], sizes[2:2 + 2 * couples:2]
    slack = jnp.minimum(source_of - 1, bound - taker)
    moved = jax.random.randint(jax.random.fold_in(rng, 1), (couples,), 0, 1 << 20) % (slack + 1)
    sizes = sizes.at[1:1 + 2 * couples:2].set(source_of - moved).at[2:2 + 2 * couples:2].set(taker + moved)
    return sizes[jax.random.permutation(jax.random.fold_in(rng, 2), amount)]


def centred(key, shape, scale, limit, pieces=(), dtype=jnp.bfloat16):
    factor_of = steps_of(key, shape, pieces, -0.22, 0.18) if pieces else 1.0
    array = jax.random.normal(key, shape, jnp.float32) * scale * factor_of
    return jnp.minimum(jnp.maximum(array, -limit), limit).astype(dtype)


def noise_with(key, dims, spread, most, shards, heavy, kind=jnp.bfloat16):
    values = spread * jax.random.normal(key, dims, jnp.float32)
    if shards:
        values = values * steps_of(key, dims, shards, -0.22, 0.18)
    return jnp.clip(with_spikes(values, jax.random.fold_in(key, 3), *heavy), -most, most).astype(kind)


def setup_inputs(seed: int = 0) -> dict:
    arg_keys = jax.random.split(jax.random.key(seed), 8)
    tokens = centred(arg_keys[0], (TOKENS, MODEL_WIDTH), 1.0, 6.0, ((0, 128), (1, 2)))
    q_weight = centred(arg_keys[1], (MODEL_WIDTH, QUERY_HEADS * HEAD_SIZE), MODEL_WIDTH ** -0.5, 0.125, ((1, 2),))
    key_matrix = centred(arg_keys[2], (MODEL_WIDTH, KEY_VALUE_HEADS * HEAD_SIZE), MODEL_WIDTH ** -0.5, 0.125, ((1, 2),))
    value_matrix = centred(arg_keys[3], (MODEL_WIDTH, KEY_VALUE_HEADS * HEAD_SIZE), MODEL_WIDTH ** -0.5, 0.125, ((1, 2),))
    norm_gain = jnp.clip(1.0 + 0.18 * jax.random.normal(arg_keys[4], (QUERY_HEADS * HEAD_SIZE,), jnp.float32), 0.1, 1.9)
    out_weight = noise_with(arg_keys[5], (QUERY_HEADS * HEAD_SIZE, MODEL_WIDTH), (QUERY_HEADS * HEAD_SIZE) ** -0.5, 0.1875, ((0, 2),), (0, 1, 2, 2.0))
    doc_ids = jnp.searchsorted(jnp.cumsum(ragged_sizes(arg_keys[6], DOCS, TOKENS, MOST_DOC, 2)), jnp.arange(TOKENS), side="right").astype(jnp.int32)
    return {"tokens": tokens, "q_weight": q_weight, "key_matrix": key_matrix, "value_matrix": value_matrix, "norm_gain": norm_gain, "out_weight": out_weight, "doc_ids": doc_ids}


epsilon = 1e-05

def features(values_in):
    return jax.nn.elu(values_in) + 1.0

def reference(tokens, q_weight, key_matrix, value_matrix, norm_gain, out_weight, doc_ids):
    query_group_width = QUERY_HEADS // KEY_VALUE_HEADS
    block_total_count = TOKENS // TOKENS_PER_SHARD
    query_rows = features(jnp.dot(tokens, q_weight, preferred_element_type=jnp.float32)).astype(jnp.bfloat16)
    key_rows = features(jnp.dot(tokens, key_matrix, preferred_element_type=jnp.float32)).astype(jnp.bfloat16)
    value_rows = jnp.dot(tokens, value_matrix, preferred_element_type=jnp.float32).astype(jnp.bfloat16)
    query_rows = query_rows.reshape(block_total_count, TOKENS_PER_SHARD, KEY_VALUE_HEADS, query_group_width, HEAD_SIZE)
    key_rows = key_rows.reshape(block_total_count, TOKENS_PER_SHARD, KEY_VALUE_HEADS, HEAD_SIZE)
    value_rows = value_rows.reshape(block_total_count, TOKENS_PER_SHARD, KEY_VALUE_HEADS, HEAD_SIZE)
    block_ids = doc_ids.reshape(block_total_count, TOKENS_PER_SHARD)
    offsets = jnp.arange(TOKENS_PER_SHARD)
    causal = offsets[:, None] >= offsets[None, :]

    def block_step(carried, block_item):
        state_sum, held_doc = carried
        block_query, block_key, block_value, block_doc = block_item
        first_id = block_doc[0]
        last_id = block_doc[TOKENS_PER_SHARD - 1]
        incoming = jnp.where(held_doc == first_id, state_sum, jnp.zeros_like(state_sum))
        same_doc = causal & (block_doc[:, None] == block_doc[None, :])
        query_wide = block_query.astype(jnp.float32)
        key_wide = block_key.astype(jnp.float32)
        value_wide = block_value.astype(jnp.float32)
        scores = jnp.einsum('tkgd,skd->kgts', query_wide, key_wide)
        scores = jnp.where(same_doc[None, None], scores, 0.0).astype(jnp.bfloat16)
        scores = lax.optimization_barrier(scores).astype(jnp.float32)
        intra_part = jnp.einsum('kgts,skd->tkgd', scores, value_wide)
        incoming_bf = lax.optimization_barrier(incoming.astype(jnp.bfloat16)).astype(jnp.float32)
        carried_part = jnp.einsum('tkgd,kde->tkge', query_wide, incoming_bf)
        carried_part = jnp.where((block_doc == first_id)[:, None, None, None], carried_part, 0.0)
        combined = (intra_part + carried_part).reshape(TOKENS_PER_SHARD, QUERY_HEADS, HEAD_SIZE)
        inv_rms = lax.rsqrt(lax.optimization_barrier(jnp.mean(combined * combined, axis=-1, keepdims=True)) + epsilon)
        normed = ((combined * inv_rms).reshape(TOKENS_PER_SHARD, QUERY_HEADS * HEAD_SIZE) * norm_gain).astype(jnp.bfloat16)
        tail_keys = jnp.where((block_doc == last_id)[:, None, None], key_wide, 0.0)
        tail_state = jnp.einsum('skd,ske->kde', tail_keys, value_wide)
        new_state = tail_state + jnp.where(last_id == first_id, incoming, jnp.zeros_like(incoming))
        return ((new_state, last_id), normed)
    starting_state = (jnp.zeros((KEY_VALUE_HEADS, HEAD_SIZE, HEAD_SIZE), jnp.float32), jnp.int32(-1))
    unused, normed_all = lax.scan(block_step, starting_state, (query_rows, key_rows, value_rows, block_ids))
    normed_all = normed_all.reshape(TOKENS, QUERY_HEADS * HEAD_SIZE)
    return jnp.dot(normed_all, out_weight, preferred_element_type=jnp.float32).astype(jnp.bfloat16)
```

```python
import jax
import jax.numpy as jnp
from jax import lax
from jax.sharding import PartitionSpec as P

HEAD_SIZE = 128
ID_ROWS = 16
ROUNDS = ((1,), (2, 4, 6), (8, 16, 24), (32, 64, 96))

epsilon = 1e-05


def features(values_in):
    return jax.nn.elu(values_in) + 1.0


def swap_head(x):
    return lax.ppermute(x, "head", [(0, 1), (1, 0)])


def carried_state(tail_state, first_id, last_id):
    place = lax.axis_index("seq")
    count = lax.axis_size("seq")
    rows = tail_state.shape[0]
    first = jnp.broadcast_to(first_id.astype(jnp.bfloat16), (1, HEAD_SIZE))
    total_id = jnp.broadcast_to(last_id.astype(jnp.bfloat16), (1, HEAD_SIZE))
    total = tail_state.astype(jnp.bfloat16)
    held = jnp.zeros((rows, HEAD_SIZE), jnp.float32)
    for bits in ROUNDS:
        message = jnp.concatenate([total, jnp.broadcast_to(total_id, (ID_ROWS, HEAD_SIZE))])
        got = [lax.ppermute(message, "seq", [(i, i ^ b) for i in range(count)]) for b in bits]
        ids = [g[rows : rows + 1] for g in got]
        top = total_id
        for i in ids:
            top = jnp.maximum(top, i)
        new = jnp.where(total_id == top, total, 0).astype(jnp.float32)
        for b, g, i in zip(bits, got, ids):
            state = g[:rows].astype(jnp.float32)
            earlier = (place & (1 << (b.bit_length() - 1))) != 0
            held = held + jnp.where((i == first) & earlier, state, 0.0)
            new = new + jnp.where(i == top, state, 0.0)
        total, total_id = new.astype(jnp.bfloat16), top
    return held


def on_device(tokens, q_weight, key_matrix, value_matrix, norm_gain, out_weight, doc_ids):
    row_count = tokens.shape[0]
    half = tokens.shape[1]
    q_heads = q_weight.shape[1] // HEAD_SIZE
    kv_heads = key_matrix.shape[1] // HEAD_SIZE
    query_group_width = q_heads // kv_heads
    core = lax.axis_index("head")
    other = swap_head(tokens)
    part_rows = jnp.where(
        core == 0,
        jnp.concatenate([tokens, other], axis=1),
        jnp.concatenate([other, tokens], axis=1),
    )
    raw_key = jnp.dot(part_rows, key_matrix, preferred_element_type=jnp.float32)
    raw_value = jnp.dot(part_rows, value_matrix, preferred_element_type=jnp.float32)
    raw_query = jnp.dot(part_rows, q_weight, preferred_element_type=jnp.float32)
    query_rows = (
        features(raw_query)
        .astype(jnp.bfloat16)
        .reshape(row_count, kv_heads, query_group_width, HEAD_SIZE)
    )
    key_rows = features(raw_key).astype(jnp.bfloat16).reshape(row_count, kv_heads, HEAD_SIZE)
    value_rows = raw_value.astype(jnp.bfloat16).reshape(row_count, kv_heads, HEAD_SIZE)
    first_id = doc_ids[0]
    last_id = doc_ids[row_count - 1]
    tail_keys = jnp.where((doc_ids == last_id)[:, None, None], key_rows, jnp.zeros_like(key_rows))
    tail_state = jnp.einsum(
        "skd,ske->kde", tail_keys, value_rows, preferred_element_type=jnp.float32
    )
    incoming = carried_state(tail_state.reshape(kv_heads * HEAD_SIZE, HEAD_SIZE), first_id, last_id)
    incoming = incoming.reshape(kv_heads, HEAD_SIZE, HEAD_SIZE)
    offsets = jnp.arange(row_count)
    same_doc = (offsets[:, None] >= offsets[None, :]) & (doc_ids[:, None] == doc_ids[None, :])
    scores = jnp.einsum("tkgd,skd->kgts", query_rows, key_rows, preferred_element_type=jnp.float32)
    scores = jnp.where(same_doc[None, None], scores, 0.0).astype(jnp.bfloat16)
    intra_part = jnp.einsum(
        "kgts,skd->tkgd", scores, value_rows, preferred_element_type=jnp.float32
    )
    carried_part = jnp.einsum(
        "tkgd,kde->tkge",
        query_rows,
        incoming.astype(jnp.bfloat16),
        preferred_element_type=jnp.float32,
    )
    carried_part = jnp.where((doc_ids == first_id)[:, None, None, None], carried_part, 0.0)
    combined = (intra_part + carried_part).reshape(row_count, q_heads, HEAD_SIZE)
    inv_rms = lax.rsqrt(jnp.mean(combined * combined, axis=-1, keepdims=True) + epsilon)
    normed = ((combined * inv_rms).reshape(row_count, q_heads * HEAD_SIZE) * norm_gain).astype(
        jnp.bfloat16
    )
    theirs = jnp.dot(
        normed,
        lax.dynamic_slice_in_dim(out_weight, (1 - core) * half, half, 1),
        preferred_element_type=jnp.float32,
    )
    received = swap_head(theirs.astype(jnp.bfloat16))
    mine = jnp.dot(
        normed,
        lax.dynamic_slice_in_dim(out_weight, core * half, half, 1),
        preferred_element_type=jnp.float32,
    )
    return (mine + received.astype(jnp.float32)).astype(jnp.bfloat16)


def solution(mesh):
    return jax.shard_map(
        on_device,
        mesh=mesh,
        in_specs=(
            P("seq", "head"),
            P(None, "head"),
            P(None, "head"),
            P(None, "head"),
            P("head"),
            P("head", None),
            P("seq"),
        ),
        out_specs=P("seq", "head"),
        check_vma=False,
    )
```

```python
import jax
import jax.numpy as jnp
from jax import lax
from jax.experimental import pallas as pl
from jax.experimental.pallas import tpu as pltpu
from jax.sharding import PartitionSpec as P

HEAD = 128
ID_ROWS = 16
BLOCK = 256
ROUNDS = ((1,), (2, 4, 6), (8, 16, 24), (32, 64, 96))
INTRA_STEPS = (1, 2)
EPSILON = 1e-05
F32 = jnp.float32
BF16 = jnp.bfloat16

SMEM = pl.BlockSpec(memory_space=pltpu.SMEM)
VMEM = pl.BlockSpec(memory_space=pltpu.VMEM)


def params(mib):
    return pltpu.CompilerParams(vmem_limit_bytes=mib << 20)


def dot(a, b):
    return jnp.dot(a, b, preferred_element_type=F32)


def features(x):
    return jnp.where(x > 0.0, x + 1.0, jnp.exp(jnp.minimum(x, 0.0)))


def project(core_ref, own_ref, other_ref, weight_ref):
    half = own_ref.shape[1]
    mine = pl.multiple_of(core_ref[0] * half, half)
    theirs = pl.multiple_of((1 - core_ref[0]) * half, half)
    return dot(own_ref[...], weight_ref[pl.ds(mine, half), :]) + dot(
        other_ref[...], weight_ref[pl.ds(theirs, half), :]
    )


def key_value_kernel(core_ref, own_ref, other_ref, wk_ref, wv_ref, col_ref, k_ref, v_ref, message_ref):
    rows = own_ref.shape[0]
    key = features(project(core_ref, own_ref, other_ref, wk_ref)).astype(BF16)
    value = project(core_ref, own_ref, other_ref, wv_ref).astype(BF16)
    k_ref[...] = key
    v_ref[...] = value
    last = col_ref[rows - 1 : rows, :]
    tail = col_ref[...] == last
    heads = key.shape[1] // HEAD
    for h in range(heads):
        cut = slice(h * HEAD, (h + 1) * HEAD)
        tail_key = jnp.where(tail, key[:, cut].astype(F32), 0.0).astype(BF16)
        state = lax.dot_general(
            tail_key, value[:, cut], (((0,), (0,)), ((), ())), preferred_element_type=F32
        )
        message_ref[cut, :] = state.astype(BF16)
    message_ref[heads * HEAD :, :] = jnp.broadcast_to(last, (ID_ROWS, HEAD)).astype(BF16)


def intra_kernel(core_ref, own_ref, other_ref, wq_ref, k_ref, v_ref, col_ref, row_ref, q_ref, intra_ref):
    rows = own_ref.shape[0]
    group = wq_ref.shape[1] // HEAD
    q_ref[...] = features(project(core_ref, own_ref, other_ref, wq_ref)).astype(BF16)
    for start in range(0, rows, BLOCK):
        seen = start + BLOCK
        here = slice(start, seen)
        key = k_ref[:seen, :]
        value = v_ref[:seen, :]
        t = lax.broadcasted_iota(jnp.int32, (BLOCK, seen), 0) + start
        s = lax.broadcasted_iota(jnp.int32, (BLOCK, seen), 1)
        same = (col_ref[here, :1] == row_ref[:1, :seen]) & (t >= s)
        for g in range(group):
            cut = slice(g * HEAD, (g + 1) * HEAD)
            scores = lax.dot_general(
                q_ref[here, cut], key, (((1,), (1,)), ((), ())), preferred_element_type=F32
            )
            scores = jnp.where(same, scores, 0.0).astype(BF16)
            intra_ref[here, cut] = dot(scores, value)


def combine_kernel(bits, has_held, place_ref, first_ref, message_ref, *refs):
    got = refs[: len(bits)]
    held_in = refs[len(bits)] if has_held else None
    next_ref, held_ref = refs[-2:]
    rows = message_ref.shape[0] - ID_ROWS
    own_id = message_ref[rows : rows + 1, :].astype(F32)
    ids = [g[rows : rows + 1, :].astype(F32) for g in got]
    top = own_id
    for i in ids:
        top = jnp.maximum(top, i)
    first = first_ref[:1, :]
    total = jnp.where(own_id == top, message_ref[:rows, :].astype(F32), 0.0)
    held = held_in[...] if has_held else jnp.zeros((rows, HEAD), F32)
    for b, g, i in zip(bits, got, ids):
        state = g[:rows, :].astype(F32)
        earlier = (place_ref[0] & (1 << (b.bit_length() - 1))) != 0
        held = held + jnp.where((i == first) & earlier, state, 0.0)
        total = total + jnp.where(i == top, state, 0.0)
    next_ref[:rows, :] = total.astype(BF16)
    next_ref[rows:, :] = jnp.broadcast_to(top, (ID_ROWS, HEAD)).astype(BF16)
    held_ref[...] = held


def norm_kernel(bits, groups, core_ref, place_ref, first_ref, held_ref, *refs):
    got = refs[: len(bits)]
    queries = refs[len(bits) : len(bits) + groups]
    intras = refs[len(bits) + groups : len(bits) + 2 * groups]
    col_ref, gain_ref, weight_ref, normed_ref, theirs_ref = refs[len(bits) + 2 * groups :]
    first = first_ref[:1, :]
    rows = held_ref.shape[0]
    held = held_ref[...]
    for b, g in zip(bits, got):
        earlier = (place_ref[0] & (1 << (b.bit_length() - 1))) != 0
        same = (g[rows : rows + 1, :].astype(F32) == first) & earlier
        held = held + jnp.where(same, g[:rows, :].astype(F32), 0.0)
    incoming = held.astype(BF16)
    for start in range(0, col_ref.shape[0], BLOCK):
        here = slice(start, start + BLOCK)
        joins = col_ref[here, :] == first
        for k in range(groups):
            width = queries[k].shape[1]
            for g in range(width // HEAD):
                cut = slice(g * HEAD, (g + 1) * HEAD)
                out = slice(k * width + g * HEAD, k * width + (g + 1) * HEAD)
                carried = dot(queries[k][here, cut], incoming[k * HEAD : (k + 1) * HEAD, :])
                combined = intras[k][here, cut] + jnp.where(joins, carried, 0.0)
                scale = lax.rsqrt(jnp.mean(combined * combined, axis=-1, keepdims=True) + EPSILON)
                normed_ref[here, out] = (combined * scale * gain_ref[:1, out]).astype(BF16)
        theirs_ref[here, :] = dot(normed_ref[here, :], columns(weight_ref, 1 - core_ref[0])).astype(BF16)


def columns(weight_ref, part):
    half = weight_ref.shape[1] // 2
    return weight_ref[:, pl.ds(pl.multiple_of(part * half, half), half)]


def own_kernel(core_ref, normed_ref, weight_ref, out_ref):
    out_ref[...] = dot(normed_ref[...], columns(weight_ref, core_ref[0]))


def shape(dims, dtype):
    return jax.ShapeDtypeStruct(dims, dtype)


def swap_head(x):
    return lax.ppermute(x, "head", [(0, 1), (1, 0)])


def on_device(tokens, q_weight, key_matrix, value_matrix, norm_gain, out_weight, doc_ids):
    rows, half = tokens.shape
    kv_width = key_matrix.shape[1]
    q_width = q_weight.shape[1]
    kv_heads = kv_width // HEAD
    group_width = q_width // kv_heads
    state_rows = kv_heads * HEAD
    count = lax.axis_size("seq")
    core = lax.axis_index("head").astype(jnp.int32).reshape(1)
    place = lax.axis_index("seq").astype(jnp.int32).reshape(1)
    other = swap_head(tokens)
    ids = doc_ids.astype(F32)
    col = jnp.broadcast_to(ids[:, None], (rows, HEAD))
    row = jnp.broadcast_to(ids[None, :], (8, rows))
    first = jnp.broadcast_to(ids[:1, None], (8, HEAD))
    gain = jnp.broadcast_to(norm_gain[None, :], (8, q_width))

    key, value, message = pl.pallas_call(
        key_value_kernel,
        out_shape=(
            shape((rows, kv_width), BF16),
            shape((rows, kv_width), BF16),
            shape((state_rows + ID_ROWS, HEAD), BF16),
        ),
        in_specs=[SMEM] + [VMEM] * 5,
        out_specs=(VMEM, VMEM, VMEM),
        compiler_params=params(24),
        name="key_value",
    )(core, tokens, other, key_matrix, value_matrix, col)

    def intra(k, key, value):
        return pl.pallas_call(
            intra_kernel,
            out_shape=(shape((rows, group_width), BF16), shape((rows, group_width), F32)),
            grid=(1,),
            in_specs=[
                SMEM,
                VMEM,
                VMEM,
                pl.BlockSpec((2 * half, group_width), lambda i: (0, k)),
                pl.BlockSpec((rows, HEAD), lambda i: (0, k)),
                pl.BlockSpec((rows, HEAD), lambda i: (0, k)),
                VMEM,
                VMEM,
            ],
            out_specs=(VMEM, VMEM),
            compiler_params=params(24),
            name=f"intra_{k}",
        )(core, tokens, other, q_weight, key, value, col, row)

    held = None
    queries, intras = [], []
    for step, bits in enumerate(ROUNDS):
        got = [lax.ppermute(message, "seq", [(i, i ^ b) for i in range(count)]) for b in bits]
        if step in INTRA_STEPS:
            (key, value), _ = lax.optimization_barrier(((key, value), message))
            query, part = intra(INTRA_STEPS.index(step), key, value)
            queries.append(query)
            intras.append(part)
        if step == len(ROUNDS) - 1:
            break
        extra = () if held is None else (held,)
        message, held = pl.pallas_call(
            lambda *refs, bits=bits, has=held is not None: combine_kernel(bits, has, *refs),
            out_shape=(shape(message.shape, BF16), shape((state_rows, HEAD), F32)),
            in_specs=[SMEM] + [VMEM] * (2 + len(bits) + len(extra)),
            out_specs=(VMEM, VMEM),
            compiler_params=params(4),
            name="combine",
        )(place, first, message, *got, *extra)
        if step in INTRA_STEPS:
            message, queries[-1] = lax.optimization_barrier((message, queries[-1]))

    normed, theirs = pl.pallas_call(
        lambda *refs: norm_kernel(ROUNDS[-1], kv_heads, *refs),
        out_shape=(shape((rows, q_width), BF16), shape((rows, half), BF16)),
        in_specs=[SMEM, SMEM] + [VMEM] * (2 + len(got) + 2 * kv_heads + 3),
        out_specs=(VMEM, VMEM),
        compiler_params=params(32),
        name="norm",
    )(core, place, first, held, *got, *queries, *intras, col, gain, out_weight)
    received = swap_head(theirs)
    mine = pl.pallas_call(
        own_kernel,
        out_shape=shape((rows, half), F32),
        in_specs=[SMEM, VMEM, VMEM],
        out_specs=VMEM,
        compiler_params=params(32),
        name="own",
    )(core, normed, out_weight)
    return (mine + received.astype(F32)).astype(BF16)


def solution(mesh):
    return jax.shard_map(
        on_device,
        mesh=mesh,
        in_specs=(
            P("seq", "head"),
            P(None, "head"),
            P(None, "head"),
            P(None, "head"),
            P("head"),
            P("head", None),
            P("seq"),
        ),
        out_specs=P("seq", "head"),
        check_vma=False,
    )
```

```python
import jax
import jax.numpy as jnp
from jax import lax
from jax.experimental import pallas as pl
from jax.experimental.pallas import tpu as pltpu
from jax.sharding import PartitionSpec as P

HEAD = 128
ID_ROWS = 16
BLOCK = 256
ROUNDS = ((1,), (2, 6, 4), (8, 24, 16), (32, 96, 64))
INTRA_STEPS = (1, 2)
CHUNKS = 2
EPSILON = 1e-05
F32 = jnp.float32
BF16 = jnp.bfloat16

SMEM = pl.BlockSpec(memory_space=pltpu.SMEM)
VMEM = pl.BlockSpec(memory_space=pltpu.VMEM)
HBM = pl.BlockSpec(memory_space=pltpu.HBM)


def params(mib):
    return pltpu.CompilerParams(vmem_limit_bytes=mib << 20)


def dot(a, b):
    return jnp.dot(a, b, preferred_element_type=F32)


def features(x):
    return jnp.where(x > 0.0, x + 1.0, jnp.exp(jnp.minimum(x, 0.0)))


def project(core_ref, own_ref, other_ref, weight_ref):
    half = own_ref.shape[1]
    mine = pl.multiple_of(core_ref[0] * half, half)
    theirs = pl.multiple_of((1 - core_ref[0]) * half, half)
    return dot(own_ref[...], weight_ref[pl.ds(mine, half), :]) + dot(
        other_ref[...], weight_ref[pl.ds(theirs, half), :]
    )


def own_half_kernel(core_ref, ids_ref, own_hbm, wk_hbm, wv_hbm, *refs):
    own_ref, wk_ref, wv_ref, k_ref, v_ref, col_ref, row_ref, sems = refs
    half = own_hbm.shape[1]
    chunk = half // CHUNKS
    near = core_ref[0] * half
    far = pl.multiple_of((1 - core_ref[0]) * half, half)
    copies = []
    for c in range(CHUNKS):
        cut = pl.ds(pl.multiple_of(near + c * chunk, chunk), chunk)
        copies.append((own_hbm.at[:, c * chunk : (c + 1) * chunk], own_ref.at[:, c * chunk : (c + 1) * chunk]))
        copies.append((wk_hbm.at[cut, :], wk_ref.at[cut, :]))
        copies.append((wv_hbm.at[cut, :], wv_ref.at[cut, :]))
    cut = pl.ds(far, half)
    copies.append((wk_hbm.at[cut, :], wk_ref.at[cut, :]))
    copies.append((wv_hbm.at[cut, :], wv_ref.at[cut, :]))
    copies = [pltpu.make_async_copy(a, b, sems.at[i]) for i, (a, b) in enumerate(copies)]
    for copy in copies:
        copy.start()
    ids = ids_ref[...].astype(F32)
    row_ref[...] = jnp.broadcast_to(ids, row_ref.shape)
    col_ref[...] = jnp.broadcast_to(ids, (HEAD, ids.shape[1])).T
    for c in range(CHUNKS):
        for copy in copies[3 * c : 3 * c + 3]:
            copy.wait()
        own = own_ref[:, c * chunk : (c + 1) * chunk]
        cut = pl.ds(pl.multiple_of(near + c * chunk, chunk), chunk)
        key = dot(own, wk_ref[cut, :])
        value = dot(own, wv_ref[cut, :])
        if c == 0:
            k_ref[...] = key
            v_ref[...] = value
        else:
            k_ref[...] += key
            v_ref[...] += value
    for copy in copies[3 * CHUNKS :]:
        copy.wait()


def key_value_kernel(core_ref, other_ref, k_part_ref, v_part_ref, wk_ref, wv_ref, col_ref, *outs):
    k_ref, v_ref, message_ref = outs
    rows, half = other_ref.shape
    other = other_ref[...]
    far = pl.ds(pl.multiple_of((1 - core_ref[0]) * half, half), half)
    key = features(k_part_ref[...] + dot(other, wk_ref[far, :])).astype(BF16)
    value = (v_part_ref[...] + dot(other, wv_ref[far, :])).astype(BF16)
    k_ref[...] = key
    v_ref[...] = value
    last = col_ref[rows - 1 : rows, :]
    tail = col_ref[...] == last
    heads = key.shape[1] // HEAD
    for h in range(heads):
        cut = slice(h * HEAD, (h + 1) * HEAD)
        tail_key = jnp.where(tail, key[:, cut].astype(F32), 0.0).astype(BF16)
        state = lax.dot_general(
            tail_key, value[:, cut], (((0,), (0,)), ((), ())), preferred_element_type=F32
        )
        message_ref[cut, :] = state.astype(BF16)
    message_ref[heads * HEAD :, :] = jnp.broadcast_to(last, (ID_ROWS, HEAD)).astype(BF16)


def intra_kernel(core_ref, own_ref, other_ref, wq_ref, k_ref, v_ref, col_ref, row_ref, q_ref, intra_ref):
    rows = own_ref.shape[0]
    group = wq_ref.shape[1] // HEAD
    q_ref[...] = features(project(core_ref, own_ref, other_ref, wq_ref)).astype(BF16)
    for start in range(0, rows, BLOCK):
        seen = start + BLOCK
        here = slice(start, seen)
        key = k_ref[:seen, :]
        value = v_ref[:seen, :]
        t = lax.broadcasted_iota(jnp.int32, (BLOCK, seen), 0) + start
        s = lax.broadcasted_iota(jnp.int32, (BLOCK, seen), 1)
        same = (col_ref[here, :1] == row_ref[:1, :seen]) & (t >= s)
        for g in range(group):
            cut = slice(g * HEAD, (g + 1) * HEAD)
            scores = lax.dot_general(
                q_ref[here, cut], key, (((1,), (1,)), ((), ())), preferred_element_type=F32
            )
            scores = jnp.where(same, scores, 0.0).astype(BF16)
            intra_ref[here, cut] = dot(scores, value)


def combine_kernel(bits, has_held, place_ref, col_ref, message_ref, *refs):
    got = refs[: len(bits)]
    held_in = refs[len(bits)] if has_held else None
    next_ref, held_ref = refs[-2:]
    rows = message_ref.shape[0] - ID_ROWS
    own_id = message_ref[rows : rows + 1, :].astype(F32)
    ids = [g[rows : rows + 1, :].astype(F32) for g in got]
    top = own_id
    for i in ids:
        top = jnp.maximum(top, i)
    first = col_ref[:1, :]
    total = jnp.where(own_id == top, message_ref[:rows, :].astype(F32), 0.0)
    held = held_in[...] if has_held else jnp.zeros((rows, HEAD), F32)
    for b, g, i in zip(bits, got, ids):
        state = g[:rows, :].astype(F32)
        earlier = (place_ref[0] & (1 << (b.bit_length() - 1))) != 0
        held = held + jnp.where((i == first) & earlier, state, 0.0)
        total = total + jnp.where(i == top, state, 0.0)
    next_ref[:rows, :] = total.astype(BF16)
    next_ref[rows:, :] = jnp.broadcast_to(top, (ID_ROWS, HEAD)).astype(BF16)
    held_ref[...] = held


def incoming_of(bits, place_ref, col_ref, held_ref, got):
    first = col_ref[:1, :]
    rows = held_ref.shape[0]
    held = held_ref[...]
    for b, g in zip(bits, got):
        earlier = (place_ref[0] & (1 << (b.bit_length() - 1))) != 0
        same = (g[rows : rows + 1, :].astype(F32) == first) & earlier
        held = held + jnp.where(same, g[:rows, :].astype(F32), 0.0)
    return held.astype(BF16)


def norm_kernel(bits, groups, core_ref, place_ref, held_ref, *refs):
    got, refs = refs[: len(bits)], refs[len(bits) :]
    queries, intras, refs = refs[:groups], refs[groups : 2 * groups], refs[2 * groups :]
    col_ref, gain_ref, weight_ref, normed_ref, theirs_ref = refs
    incoming = incoming_of(bits, place_ref, col_ref, held_ref, got)
    for start in range(0, col_ref.shape[0], BLOCK):
        here = slice(start, start + BLOCK)
        joins = col_ref[here, :] == col_ref[:1, :]
        for k in range(groups):
            width = queries[k].shape[1]
            for g in range(width // HEAD):
                cut = slice(g * HEAD, (g + 1) * HEAD)
                out = slice(k * width + g * HEAD, k * width + (g + 1) * HEAD)
                carried = dot(queries[k][here, cut], incoming[k * HEAD : (k + 1) * HEAD, :])
                combined = intras[k][here, cut] + jnp.where(joins, carried, 0.0)
                scale = lax.rsqrt(jnp.mean(combined * combined, axis=-1, keepdims=True) + EPSILON)
                normed_ref[here, out] = (combined * scale * gain_ref[:1, out]).astype(BF16)
        theirs_ref[here, :] = dot(normed_ref[here, :], columns(weight_ref, 1 - core_ref[0])).astype(BF16)


def columns(weight_ref, part):
    half = weight_ref.shape[1] // 2
    return weight_ref[:, pl.ds(pl.multiple_of(part * half, half), half)]


def own_kernel(core_ref, normed_ref, weight_ref, out_ref):
    out_ref[...] = dot(normed_ref[...], columns(weight_ref, core_ref[0]))


def add_kernel(mine_ref, theirs_ref, out_ref):
    size = out_ref.shape[0]
    here = pl.ds(pl.multiple_of(pl.program_id(0) * size, size), size)
    out_ref[...] = (mine_ref[here, :] + theirs_ref[here, :].astype(F32)).astype(BF16)


def shape(dims, dtype):
    return jax.ShapeDtypeStruct(dims, dtype)


def in_hbm(x):
    return pltpu.with_memory_space_constraint(x, pltpu.HBM)


def swap_head(x):
    return lax.ppermute(x, "head", [(0, 1), (1, 0)])


def on_device(tokens, q_weight, key_matrix, value_matrix, norm_gain, out_weight, doc_ids):
    rows, half = tokens.shape
    kv_width = key_matrix.shape[1]
    q_width = q_weight.shape[1]
    kv_heads = kv_width // HEAD
    group_width = q_width // kv_heads
    state_rows = kv_heads * HEAD
    count = lax.axis_size("seq")
    core = lax.axis_index("head").astype(jnp.int32).reshape(1)
    place = lax.axis_index("seq").astype(jnp.int32).reshape(1)
    other = swap_head(tokens)
    gain = norm_gain.reshape(1, q_width)
    own, wk, wv, k_part, v_part, col, row = pl.pallas_call(
        own_half_kernel,
        out_shape=(
            shape(tokens.shape, BF16),
            shape(key_matrix.shape, BF16),
            shape(value_matrix.shape, BF16),
            shape((rows, kv_width), F32),
            shape((rows, kv_width), F32),
            shape((rows, HEAD), F32),
            shape((8, rows), F32),
        ),
        in_specs=[SMEM, VMEM, HBM, HBM, HBM],
        out_specs=(VMEM,) * 7,
        scratch_shapes=[pltpu.SemaphoreType.DMA((3 * CHUNKS + 2,))],
        compiler_params=params(8),
        name="own_half",
    )(core, doc_ids.reshape(1, rows), *(in_hbm(x) for x in (tokens, key_matrix, value_matrix)))

    key, value, message = pl.pallas_call(
        key_value_kernel,
        out_shape=(
            shape((rows, kv_width), BF16),
            shape((rows, kv_width), BF16),
            shape((state_rows + ID_ROWS, HEAD), BF16),
        ),
        in_specs=[SMEM] + [VMEM] * 6,
        out_specs=(VMEM, VMEM, VMEM),
        compiler_params=params(16),
        name="key_value",
    )(core, other, k_part, v_part, wk, wv, col)

    def intra(k, key, value):
        return pl.pallas_call(
            intra_kernel,
            out_shape=(shape((rows, group_width), BF16), shape((rows, group_width), F32)),
            grid=(1,),
            in_specs=[
                SMEM,
                VMEM,
                VMEM,
                pl.BlockSpec((2 * half, group_width), lambda i: (0, k)),
                pl.BlockSpec((rows, HEAD), lambda i: (0, k)),
                pl.BlockSpec((rows, HEAD), lambda i: (0, k)),
                VMEM,
                VMEM,
            ],
            out_specs=(VMEM, VMEM),
            compiler_params=params(24),
            name=f"intra_{k}",
        )(core, own, other, q_weight, key, value, col, row)

    held = None
    queries, intras = [], []
    for step, bits in enumerate(ROUNDS):
        final = step == len(ROUNDS) - 1
        got = [
            lax.ppermute(message, "seq", [(i, i ^ b) for i in range(count) if i < i ^ b or not final])
            for b in bits
        ]
        if step in INTRA_STEPS:
            (key, value), _ = lax.optimization_barrier(((key, value), message))
            query, part = intra(INTRA_STEPS.index(step), key, value)
            queries.append(query)
            intras.append(part)
        if final:
            break
        extra = () if held is None else (held,)
        message, held = pl.pallas_call(
            lambda *refs, bits=bits, has=held is not None: combine_kernel(bits, has, *refs),
            out_shape=(shape(message.shape, BF16), shape((state_rows, HEAD), F32)),
            in_specs=[SMEM] + [VMEM] * (2 + len(bits) + len(extra)),
            out_specs=(VMEM, VMEM),
            compiler_params=params(4),
            name="combine",
        )(place, col, message, *got, *extra)
        if step in INTRA_STEPS:
            message, queries[-1] = lax.optimization_barrier((message, queries[-1]))

    normed, theirs = pl.pallas_call(
        lambda *refs: norm_kernel(ROUNDS[-1], kv_heads, *refs),
        out_shape=(shape((rows, q_width), BF16), shape((rows, half), BF16)),
        in_specs=[SMEM, SMEM] + [VMEM] * (1 + len(got) + 2 * kv_heads + 3),
        out_specs=(VMEM, VMEM),
        compiler_params=params(16),
        name="norm",
    )(core, place, held, *got, *queries, *intras, col, gain, out_weight)
    received = swap_head(theirs)
    mine = pl.pallas_call(
        own_kernel,
        out_shape=shape((rows, half), F32),
        in_specs=[SMEM, VMEM, VMEM],
        out_specs=VMEM,
        compiler_params=params(16),
        name="own",
    )(core, normed, out_weight)
    return pl.pallas_call(
        add_kernel,
        grid=(4,),
        out_shape=shape((rows, half), BF16),
        in_specs=[VMEM, VMEM],
        out_specs=pl.BlockSpec((rows // 4, half), lambda i: (i, 0)),
        compiler_params=params(8),
        name="add",
    )(mine, received)


def solution(mesh):
    return jax.shard_map(
        on_device,
        mesh=mesh,
        in_specs=(
            P("seq", "head"),
            P(None, "head"),
            P(None, "head"),
            P(None, "head"),
            P("head"),
            P("head", None),
            P("seq"),
        ),
        out_specs=P("seq", "head"),
        check_vma=False,
    )
```

```python
import jax
import jax.numpy as jnp
from jax import lax
from jax.experimental import pallas as pl
from jax.experimental.pallas import tpu as pltpu
from jax.sharding import PartitionSpec as P

HEAD = 128
ID_ROWS = 16
BLOCK = 256
ROUNDS = ((1,), (2, 6, 4), (8, 24, 16), (32, 96, 64))
INTRA_STEPS = (1, 2)
CHUNKS = 2
STAGE_COPIES = 4
ADD_STEPS = 2
EPSILON = 1e-05
F32 = jnp.float32
BF16 = jnp.bfloat16

SMEM = pl.BlockSpec(memory_space=pltpu.SMEM)
VMEM = pl.BlockSpec(memory_space=pltpu.VMEM)
HBM = pl.BlockSpec(memory_space=pltpu.HBM)


def params(mib):
    return pltpu.CompilerParams(vmem_limit_bytes=mib << 20)


def dot(a, b):
    return jnp.dot(a, b, preferred_element_type=F32)


def features(x):
    return jnp.where(x > 0.0, x + 1.0, jnp.exp(jnp.minimum(x, 0.0)))


def project(core_ref, own_ref, other_ref, weight_ref):
    half = own_ref.shape[1]
    mine = pl.multiple_of(core_ref[0] * half, half)
    theirs = pl.multiple_of((1 - core_ref[0]) * half, half)
    return dot(own_ref[...], weight_ref[pl.ds(mine, half), :]) + dot(
        other_ref[...], weight_ref[pl.ds(theirs, half), :]
    )


def own_half_kernel(core_ref, ids_hbm, own_hbm, wk_hbm, wv_hbm, *refs):
    own_ref, wk_ref, wv_ref, k_ref, v_ref, col_ref, row_ref, ids_vmem, sems = refs
    half = own_hbm.shape[1]
    chunk = half // CHUNKS
    near = core_ref[0] * half
    far = pl.multiple_of((1 - core_ref[0]) * half, half)
    copies = []
    for c in range(CHUNKS):
        cut = pl.ds(pl.multiple_of(near + c * chunk, chunk), chunk)
        copies.append((own_hbm.at[:, c * chunk : (c + 1) * chunk], own_ref.at[:, c * chunk : (c + 1) * chunk]))
        copies.append((wk_hbm.at[cut, :], wk_ref.at[cut, :]))
        copies.append((wv_hbm.at[cut, :], wv_ref.at[cut, :]))
    cut = pl.ds(far, half)
    copies.append((wk_hbm.at[cut, :], wk_ref.at[cut, :]))
    copies.append((wv_hbm.at[cut, :], wv_ref.at[cut, :]))
    copies.insert(0, (ids_hbm, ids_vmem))
    copies = [pltpu.make_async_copy(a, b, sems.at[i]) for i, (a, b) in enumerate(copies)]
    for copy in copies:
        copy.start()
    copies[0].wait()
    ids = ids_vmem[...].astype(F32)
    row_ref[...] = jnp.broadcast_to(ids, row_ref.shape)
    col_ref[...] = jnp.broadcast_to(ids, (HEAD, ids.shape[1])).T
    for c in range(CHUNKS):
        for copy in copies[3 * c + 1 : 3 * c + 4]:
            copy.wait()
        own = own_ref[:, c * chunk : (c + 1) * chunk]
        cut = pl.ds(pl.multiple_of(near + c * chunk, chunk), chunk)
        key = dot(own, wk_ref[cut, :])
        value = dot(own, wv_ref[cut, :])
        if c == 0:
            k_ref[...] = key
            v_ref[...] = value
        else:
            k_ref[...] += key
            v_ref[...] += value
    for copy in copies[3 * CHUNKS + 1 :]:
        copy.wait()


def key_value_kernel(core_ref, other_ref, k_part_ref, v_part_ref, wk_ref, wv_ref, col_ref, *outs):
    k_ref, v_ref, message_ref = outs
    rows, half = other_ref.shape
    other = other_ref[...]
    far = pl.ds(pl.multiple_of((1 - core_ref[0]) * half, half), half)
    key = features(k_part_ref[...] + dot(other, wk_ref[far, :])).astype(BF16)
    value = (v_part_ref[...] + dot(other, wv_ref[far, :])).astype(BF16)
    k_ref[...] = key
    v_ref[...] = value
    last = col_ref[rows - 1 : rows, :]
    tail = col_ref[...] == last
    heads = key.shape[1] // HEAD
    for h in range(heads):
        cut = slice(h * HEAD, (h + 1) * HEAD)
        tail_key = jnp.where(tail, key[:, cut].astype(F32), 0.0).astype(BF16)
        state = lax.dot_general(
            tail_key, value[:, cut], (((0,), (0,)), ((), ())), preferred_element_type=F32
        )
        message_ref[cut, :] = state.astype(BF16)
    message_ref[heads * HEAD :, :] = jnp.broadcast_to(last, (ID_ROWS, HEAD)).astype(BF16)


def stage_kernel(after_ref, weight_hbm, weight_ref, sems):
    size = weight_ref.shape[0] // STAGE_COPIES
    copies = []
    for i in range(STAGE_COPIES):
        cut = slice(i * size, (i + 1) * size)
        copies.append(pltpu.make_async_copy(weight_hbm.at[cut, :], weight_ref.at[cut, :], sems.at[i]))
    for copy in copies:
        copy.start()
    for copy in copies:
        copy.wait()


def intra_kernel(core_ref, own_ref, other_ref, wq_ref, k_ref, v_ref, col_ref, row_ref, q_ref, intra_ref):
    rows = own_ref.shape[0]
    group = wq_ref.shape[1] // HEAD
    q_ref[...] = features(project(core_ref, own_ref, other_ref, wq_ref)).astype(BF16)
    for start in range(0, rows, BLOCK):
        seen = start + BLOCK
        here = slice(start, seen)
        key = k_ref[:seen, :]
        value = v_ref[:seen, :]
        t = lax.broadcasted_iota(jnp.int32, (BLOCK, seen), 0) + start
        s = lax.broadcasted_iota(jnp.int32, (BLOCK, seen), 1)
        same = (col_ref[here, :1] == row_ref[:1, :seen]) & (t >= s)
        for g in range(group):
            cut = slice(g * HEAD, (g + 1) * HEAD)
            scores = lax.dot_general(
                q_ref[here, cut], key, (((1,), (1,)), ((), ())), preferred_element_type=F32
            )
            scores = jnp.where(same, scores, 0.0).astype(BF16)
            intra_ref[here, cut] = dot(scores, value)


def combine_kernel(bits, has_held, place_ref, col_ref, message_ref, *refs):
    got = refs[: len(bits)]
    held_in = refs[len(bits)] if has_held else None
    next_ref, held_ref = refs[-2:]
    rows = message_ref.shape[0] - ID_ROWS
    own_id = message_ref[rows : rows + 1, :].astype(F32)
    ids = [g[rows : rows + 1, :].astype(F32) for g in got]
    top = own_id
    for i in ids:
        top = jnp.maximum(top, i)
    first = col_ref[:1, :]
    total = jnp.where(own_id == top, message_ref[:rows, :].astype(F32), 0.0)
    held = held_in[...] if has_held else jnp.zeros((rows, HEAD), F32)
    for b, g, i in zip(bits, got, ids):
        state = g[:rows, :].astype(F32)
        earlier = (place_ref[0] & (1 << (b.bit_length() - 1))) != 0
        held = held + jnp.where((i == first) & earlier, state, 0.0)
        total = total + jnp.where(i == top, state, 0.0)
    next_ref[:rows, :] = total.astype(BF16)
    next_ref[rows:, :] = jnp.broadcast_to(top, (ID_ROWS, HEAD)).astype(BF16)
    held_ref[...] = held


def incoming_of(bits, place_ref, col_ref, held_ref, got):
    first = col_ref[:1, :]
    rows = held_ref.shape[0]
    held = held_ref[...]
    for b, g in zip(bits, got):
        earlier = (place_ref[0] & (1 << (b.bit_length() - 1))) != 0
        same = (g[rows : rows + 1, :].astype(F32) == first) & earlier
        held = held + jnp.where(same, g[:rows, :].astype(F32), 0.0)
    return held.astype(BF16)


def norm_kernel(bits, groups, core_ref, place_ref, held_ref, *refs):
    got, refs = refs[: len(bits)], refs[len(bits) :]
    queries, intras, refs = refs[:groups], refs[groups : 2 * groups], refs[2 * groups :]
    col_ref, gain_ref, weight_ref, normed_ref, *theirs = refs
    incoming = incoming_of(bits, place_ref, col_ref, held_ref, got)
    for start in range(0, col_ref.shape[0], BLOCK):
        here = slice(start, start + BLOCK)
        joins = col_ref[here, :] == col_ref[:1, :]
        for k in range(groups):
            width = queries[k].shape[1]
            for g in range(width // HEAD):
                cut = slice(g * HEAD, (g + 1) * HEAD)
                out = slice(k * width + g * HEAD, k * width + (g + 1) * HEAD)
                carried = dot(queries[k][here, cut], incoming[k * HEAD : (k + 1) * HEAD, :])
                combined = intras[k][here, cut] + jnp.where(joins, carried, 0.0)
                scale = lax.rsqrt(jnp.mean(combined * combined, axis=-1, keepdims=True) + EPSILON)
                normed_ref[here, out] = (combined * scale * gain_ref[:1, out]).astype(BF16)
        theirs[start // BLOCK][...] = dot(normed_ref[here, :], columns(weight_ref, 1 - core_ref[0])).astype(BF16)


def columns(weight_ref, part):
    half = weight_ref.shape[1] // 2
    return weight_ref[:, pl.ds(pl.multiple_of(part * half, half), half)]


def own_kernel(core_ref, normed_ref, weight_ref, out_ref):
    out_ref[...] = dot(normed_ref[...], columns(weight_ref, core_ref[0]))


def add_kernel(mine_ref, theirs_ref, *refs):
    out_ref = refs[-1]
    size = out_ref.shape[0]
    step = pl.program_id(0)
    first = pl.multiple_of((step + (pl.num_programs(0) if len(refs) > 1 else 0)) * size, size)
    here = pl.ds(pl.multiple_of(step * size, size), size)
    out_ref[...] = (mine_ref[pl.ds(first, size), :] + theirs_ref[here, :].astype(F32)).astype(BF16)


def shape(dims, dtype):
    return jax.ShapeDtypeStruct(dims, dtype)


def in_hbm(x):
    return pltpu.with_memory_space_constraint(x, pltpu.HBM)


def swap_head(x):
    return lax.ppermute(x, "head", [(0, 1), (1, 0)])


def on_device(tokens, q_weight, key_matrix, value_matrix, norm_gain, out_weight, doc_ids):
    rows, half = tokens.shape
    kv_width = key_matrix.shape[1]
    q_width = q_weight.shape[1]
    kv_heads = kv_width // HEAD
    group_width = q_width // kv_heads
    state_rows = kv_heads * HEAD
    count = lax.axis_size("seq")
    core = lax.axis_index("head").astype(jnp.int32).reshape(1)
    place = lax.axis_index("seq").astype(jnp.int32).reshape(1)
    other = swap_head(tokens)
    gain = norm_gain.reshape(1, q_width)
    own, wk, wv, k_part, v_part, col, row = pl.pallas_call(
        own_half_kernel,
        out_shape=(
            shape(tokens.shape, BF16),
            shape(key_matrix.shape, BF16),
            shape(value_matrix.shape, BF16),
            shape((rows, kv_width), F32),
            shape((rows, kv_width), F32),
            shape((rows, HEAD), F32),
            shape((8, rows), F32),
        ),
        in_specs=[SMEM, HBM, HBM, HBM, HBM],
        out_specs=(VMEM,) * 7,
        scratch_shapes=[pltpu.VMEM((1, rows), jnp.int32), pltpu.SemaphoreType.DMA((3 * CHUNKS + 3,))],
        compiler_params=params(8),
        name="own_half",
    )(core, *(in_hbm(x) for x in (doc_ids.reshape(1, rows), tokens, key_matrix, value_matrix)))

    key, value, message = pl.pallas_call(
        key_value_kernel,
        out_shape=(
            shape((rows, kv_width), BF16),
            shape((rows, kv_width), BF16),
            shape((state_rows + ID_ROWS, HEAD), BF16),
        ),
        in_specs=[SMEM] + [VMEM] * 6,
        out_specs=(VMEM, VMEM, VMEM),
        compiler_params=params(16),
        name="key_value",
    )(core, other, k_part, v_part, wk, wv, col)

    def intra(k, key, value):
        return pl.pallas_call(
            intra_kernel,
            out_shape=(shape((rows, group_width), BF16), shape((rows, group_width), F32)),
            grid=(1,),
            in_specs=[
                SMEM,
                VMEM,
                VMEM,
                pl.BlockSpec((2 * half, group_width), lambda i: (0, k)),
                pl.BlockSpec((rows, HEAD), lambda i: (0, k)),
                pl.BlockSpec((rows, HEAD), lambda i: (0, k)),
                VMEM,
                VMEM,
            ],
            out_specs=(VMEM, VMEM),
            compiler_params=params(24),
            name=f"intra_{k}",
        )(core, own, other, wq, key, value, col, row)

    held = None
    queries, intras = [], []
    for step, bits in enumerate(ROUNDS):
        final = step == len(ROUNDS) - 1
        got = [lax.ppermute(message, "seq", [(i, i ^ b) for i in range(count)]) for b in bits]
        if step == 0:
            wq = pl.pallas_call(
                stage_kernel,
                out_shape=shape(q_weight.shape, BF16),
                in_specs=[VMEM, HBM],
                out_specs=VMEM,
                scratch_shapes=[pltpu.SemaphoreType.DMA((STAGE_COPIES,))],
                compiler_params=params(2),
                name="stage",
            )(message, in_hbm(q_weight))
        if step in INTRA_STEPS:
            (key, value), _ = lax.optimization_barrier(((key, value), message))
            query, part = intra(INTRA_STEPS.index(step), key, value)
            queries.append(query)
            intras.append(part)
        if final:
            break
        extra = () if held is None else (held,)
        message, held = pl.pallas_call(
            lambda *refs, bits=bits, has=held is not None: combine_kernel(bits, has, *refs),
            out_shape=(shape(message.shape, BF16), shape((state_rows, HEAD), F32)),
            in_specs=[SMEM] + [VMEM] * (2 + len(bits) + len(extra)),
            out_specs=(VMEM, VMEM),
            compiler_params=params(4),
            name="combine",
        )(place, col, message, *got, *extra)
        if step == 0:
            message, wq = lax.optimization_barrier((message, wq))
        if step in INTRA_STEPS:
            message, queries[-1] = lax.optimization_barrier((message, queries[-1]))

    normed, *theirs = pl.pallas_call(
        lambda *refs: norm_kernel(ROUNDS[-1], kv_heads, *refs),
        out_shape=(shape((rows, q_width), BF16),) + (shape((BLOCK, half), BF16),) * (rows // BLOCK),
        in_specs=[SMEM, SMEM] + [VMEM] * (1 + len(got) + 2 * kv_heads + 3),
        out_specs=(VMEM,) * (1 + rows // BLOCK),
        compiler_params=params(16),
        name="norm",
    )(core, place, held, *got, *queries, *intras, col, gain, out_weight)
    received = [swap_head(part) for part in theirs]
    mine = pl.pallas_call(
        own_kernel,
        out_shape=shape((rows, half), F32),
        in_specs=[SMEM, VMEM, VMEM],
        out_specs=VMEM,
        compiler_params=params(16),
        name="own",
    )(core, normed, out_weight)
    out = ()
    for part in range(rows // BLOCK):
        out = (
            pl.pallas_call(
                add_kernel,
                grid=(ADD_STEPS,),
                out_shape=shape((rows, half), BF16),
                in_specs=[VMEM, VMEM] + [HBM] * len(out),
                out_specs=pl.BlockSpec(
                    (BLOCK // ADD_STEPS, half), lambda i, part=part: (i + part * ADD_STEPS, 0)
                ),
                input_output_aliases={2: 0} if out else {},
                compiler_params=params(8),
                name=f"add_{part}",
            )(mine, received[part], *out),
        )
    return out[0]


def solution(mesh):
    return jax.shard_map(
        on_device,
        mesh=mesh,
        in_specs=(
            P("seq", "head"),
            P(None, "head"),
            P(None, "head"),
            P(None, "head"),
            P("head"),
            P("head", None),
            P("seq"),
        ),
        out_specs=P("seq", "head"),
        check_vma=False,
    )
```

```python
import jax
import jax.numpy as jnp
from jax import lax
from jax.experimental import pallas as pl
from jax.experimental.pallas import tpu as pltpu
from jax.sharding import PartitionSpec as P

HEAD = 128
ID_ROWS = 16
BLOCK = 256
ROUNDS = ((1,), (2, 6, 5), (8, 24, 16), (32, 96, 64))
INTRA_STEPS = (1, 2)
CHUNKS = 2
STAGE_COPIES = 4
ADD_STEPS = 2
EPSILON = 1e-05
F32 = jnp.float32
BF16 = jnp.bfloat16

SMEM = pl.BlockSpec(memory_space=pltpu.SMEM)
VMEM = pl.BlockSpec(memory_space=pltpu.VMEM)
HBM = pl.BlockSpec(memory_space=pltpu.HBM)


def params(mib):
    return pltpu.CompilerParams(vmem_limit_bytes=mib << 20)


def dot(a, b):
    return jnp.dot(a, b, preferred_element_type=F32)


def features(x):
    return jnp.where(x > 0.0, x + 1.0, jnp.exp(jnp.minimum(x, 0.0)))


def project(core_ref, own_ref, other_ref, weight_ref):
    half = own_ref.shape[1]
    mine = pl.multiple_of(core_ref[0] * half, half)
    theirs = pl.multiple_of((1 - core_ref[0]) * half, half)
    return dot(own_ref[...], weight_ref[pl.ds(mine, half), :]) + dot(
        other_ref[...], weight_ref[pl.ds(theirs, half), :]
    )


def own_half_kernel(core_ref, ids_hbm, own_hbm, wk_hbm, wv_hbm, *refs):
    own_ref, wk_ref, wv_ref, k_ref, v_ref, col_ref, row_ref, ids_vmem, sems = refs
    half = own_hbm.shape[1]
    chunk = half // CHUNKS
    near = core_ref[0] * half
    far = pl.multiple_of((1 - core_ref[0]) * half, half)
    copies = []
    for c in range(CHUNKS):
        cut = pl.ds(pl.multiple_of(near + c * chunk, chunk), chunk)
        copies.append((own_hbm.at[:, c * chunk : (c + 1) * chunk], own_ref.at[:, c * chunk : (c + 1) * chunk]))
        copies.append((wk_hbm.at[cut, :], wk_ref.at[cut, :]))
        copies.append((wv_hbm.at[cut, :], wv_ref.at[cut, :]))
    cut = pl.ds(far, half)
    copies.append((wk_hbm.at[cut, :], wk_ref.at[cut, :]))
    copies.append((wv_hbm.at[cut, :], wv_ref.at[cut, :]))
    copies.insert(0, (ids_hbm, ids_vmem))
    copies = [pltpu.make_async_copy(a, b, sems.at[i]) for i, (a, b) in enumerate(copies)]
    for copy in copies:
        copy.start()
    copies[0].wait()
    ids = ids_vmem[...].astype(F32)
    row_ref[...] = jnp.broadcast_to(ids, row_ref.shape)
    col_ref[...] = jnp.broadcast_to(ids, (HEAD, ids.shape[1])).T
    for c in range(CHUNKS):
        for copy in copies[3 * c + 1 : 3 * c + 4]:
            copy.wait()
        own = own_ref[:, c * chunk : (c + 1) * chunk]
        cut = pl.ds(pl.multiple_of(near + c * chunk, chunk), chunk)
        key = dot(own, wk_ref[cut, :])
        value = dot(own, wv_ref[cut, :])
        if c == 0:
            k_ref[...] = key
            v_ref[...] = value
        else:
            k_ref[...] += key
            v_ref[...] += value
    for copy in copies[3 * CHUNKS + 1 :]:
        copy.wait()


def key_value_kernel(core_ref, other_ref, k_part_ref, v_part_ref, wk_ref, wv_ref, col_ref, *outs):
    k_ref, v_ref, message_ref = outs
    rows, half = other_ref.shape
    other = other_ref[...]
    far = pl.ds(pl.multiple_of((1 - core_ref[0]) * half, half), half)
    key = features(k_part_ref[...] + dot(other, wk_ref[far, :])).astype(BF16)
    value = (v_part_ref[...] + dot(other, wv_ref[far, :])).astype(BF16)
    k_ref[...] = key
    v_ref[...] = value
    last = col_ref[rows - 1 : rows, :]
    tail = col_ref[...] == last
    heads = key.shape[1] // HEAD
    for h in range(heads):
        cut = slice(h * HEAD, (h + 1) * HEAD)
        tail_key = jnp.where(tail, key[:, cut].astype(F32), 0.0).astype(BF16)
        state = lax.dot_general(
            tail_key, value[:, cut], (((0,), (0,)), ((), ())), preferred_element_type=F32
        )
        message_ref[cut, :] = state.astype(BF16)
    message_ref[heads * HEAD :, :] = jnp.broadcast_to(last, (ID_ROWS, HEAD)).astype(BF16)


def stage_kernel(after_ref, weight_hbm, weight_ref, sems):
    size = weight_ref.shape[0] // STAGE_COPIES
    copies = []
    for i in range(STAGE_COPIES):
        cut = slice(i * size, (i + 1) * size)
        copies.append(pltpu.make_async_copy(weight_hbm.at[cut, :], weight_ref.at[cut, :], sems.at[i]))
    for copy in copies:
        copy.start()
    for copy in copies:
        copy.wait()


def intra_kernel(core_ref, own_ref, other_ref, wq_ref, k_ref, v_ref, col_ref, row_ref, q_ref, intra_ref):
    rows = own_ref.shape[0]
    group = wq_ref.shape[1] // HEAD
    q_ref[...] = features(project(core_ref, own_ref, other_ref, wq_ref)).astype(BF16)
    for start in range(0, rows, BLOCK):
        seen = start + BLOCK
        here = slice(start, seen)
        key = k_ref[:seen, :]
        value = v_ref[:seen, :]
        t = lax.broadcasted_iota(jnp.int32, (BLOCK, seen), 0) + start
        s = lax.broadcasted_iota(jnp.int32, (BLOCK, seen), 1)
        same = (col_ref[here, :1] == row_ref[:1, :seen]) & (t >= s)
        for g in range(group):
            cut = slice(g * HEAD, (g + 1) * HEAD)
            scores = lax.dot_general(
                q_ref[here, cut], key, (((1,), (1,)), ((), ())), preferred_element_type=F32
            )
            scores = jnp.where(same, scores, 0.0).astype(BF16)
            intra_ref[here, cut] = dot(scores, value)


def combine_kernel(bits, has_held, place_ref, col_ref, message_ref, *refs):
    got = refs[: len(bits)]
    held_in = refs[len(bits)] if has_held else None
    next_ref, held_ref = refs[-2:]
    rows = message_ref.shape[0] - ID_ROWS
    own_id = message_ref[rows : rows + 1, :].astype(F32)
    ids = [g[rows : rows + 1, :].astype(F32) for g in got]
    top = own_id
    for i in ids:
        top = jnp.maximum(top, i)
    first = col_ref[:1, :]
    total = jnp.where(own_id == top, message_ref[:rows, :].astype(F32), 0.0)
    held = held_in[...] if has_held else jnp.zeros((rows, HEAD), F32)
    for b, g, i in zip(bits, got, ids):
        state = g[:rows, :].astype(F32)
        earlier = (place_ref[0] & (1 << (b.bit_length() - 1))) != 0
        held = held + jnp.where((i == first) & earlier, state, 0.0)
        total = total + jnp.where(i == top, state, 0.0)
    next_ref[:rows, :] = total.astype(BF16)
    next_ref[rows:, :] = jnp.broadcast_to(top, (ID_ROWS, HEAD)).astype(BF16)
    held_ref[...] = held


def incoming_of(bits, place_ref, col_ref, held_ref, got):
    first = col_ref[:1, :]
    rows = held_ref.shape[0]
    held = held_ref[...]
    for b, g in zip(bits, got):
        earlier = (place_ref[0] & (1 << (b.bit_length() - 1))) != 0
        same = (g[rows : rows + 1, :].astype(F32) == first) & earlier
        held = held + jnp.where(same, g[:rows, :].astype(F32), 0.0)
    return held.astype(BF16)


def norm_kernel(bits, groups, core_ref, place_ref, held_ref, *refs):
    got, refs = refs[: len(bits)], refs[len(bits) :]
    queries, intras, refs = refs[:groups], refs[groups : 2 * groups], refs[2 * groups :]
    col_ref, gain_ref, weight_ref, normed_ref, *theirs = refs
    incoming = incoming_of(bits, place_ref, col_ref, held_ref, got)
    for start in range(0, col_ref.shape[0], BLOCK):
        here = slice(start, start + BLOCK)
        joins = col_ref[here, :] == col_ref[:1, :]
        for k in range(groups):
            width = queries[k].shape[1]
            for g in range(width // HEAD):
                cut = slice(g * HEAD, (g + 1) * HEAD)
                out = slice(k * width + g * HEAD, k * width + (g + 1) * HEAD)
                carried = dot(queries[k][here, cut], incoming[k * HEAD : (k + 1) * HEAD, :])
                combined = intras[k][here, cut] + jnp.where(joins, carried, 0.0)
                scale = lax.rsqrt(jnp.mean(combined * combined, axis=-1, keepdims=True) + EPSILON)
                normed_ref[here, out] = (combined * scale * gain_ref[:1, out]).astype(BF16)
        theirs[start // BLOCK][...] = dot(normed_ref[here, :], columns(weight_ref, 1 - core_ref[0])).astype(BF16)


def columns(weight_ref, part):
    half = weight_ref.shape[1] // 2
    return weight_ref[:, pl.ds(pl.multiple_of(part * half, half), half)]


def own_kernel(core_ref, normed_ref, weight_ref, out_ref):
    out_ref[...] = dot(normed_ref[...], columns(weight_ref, core_ref[0]))


def add_kernel(mine_ref, theirs_ref, *refs):
    out_ref = refs[-1]
    size = out_ref.shape[0]
    step = pl.program_id(0)
    first = pl.multiple_of((step + (pl.num_programs(0) if len(refs) > 1 else 0)) * size, size)
    here = pl.ds(pl.multiple_of(step * size, size), size)
    out_ref[...] = (mine_ref[pl.ds(first, size), :] + theirs_ref[here, :].astype(F32)).astype(BF16)


def shape(dims, dtype):
    return jax.ShapeDtypeStruct(dims, dtype)


def in_hbm(x):
    return pltpu.with_memory_space_constraint(x, pltpu.HBM)


def swap_head(x):
    return lax.ppermute(x, "head", [(0, 1), (1, 0)])


def on_device(tokens, q_weight, key_matrix, value_matrix, norm_gain, out_weight, doc_ids):
    rows, half = tokens.shape
    kv_width = key_matrix.shape[1]
    q_width = q_weight.shape[1]
    kv_heads = kv_width // HEAD
    group_width = q_width // kv_heads
    state_rows = kv_heads * HEAD
    count = lax.axis_size("seq")
    core = lax.axis_index("head").astype(jnp.int32).reshape(1)
    place = lax.axis_index("seq").astype(jnp.int32).reshape(1)
    other = swap_head(tokens)
    gain = norm_gain.reshape(1, q_width)
    own, wk, wv, k_part, v_part, col, row = pl.pallas_call(
        own_half_kernel,
        out_shape=(
            shape(tokens.shape, BF16),
            shape(key_matrix.shape, BF16),
            shape(value_matrix.shape, BF16),
            shape((rows, kv_width), F32),
            shape((rows, kv_width), F32),
            shape((rows, HEAD), F32),
            shape((8, rows), F32),
        ),
        in_specs=[SMEM, HBM, HBM, HBM, HBM],
        out_specs=(VMEM,) * 7,
        scratch_shapes=[pltpu.VMEM((1, rows), jnp.int32), pltpu.SemaphoreType.DMA((3 * CHUNKS + 3,))],
        compiler_params=params(8),
        name="own_half",
    )(core, *(in_hbm(x) for x in (doc_ids.reshape(1, rows), tokens, key_matrix, value_matrix)))

    key, value, message = pl.pallas_call(
        key_value_kernel,
        out_shape=(
            shape((rows, kv_width), BF16),
            shape((rows, kv_width), BF16),
            shape((state_rows + ID_ROWS, HEAD), BF16),
        ),
        in_specs=[SMEM] + [VMEM] * 6,
        out_specs=(VMEM, VMEM, VMEM),
        compiler_params=params(16),
        name="key_value",
    )(core, other, k_part, v_part, wk, wv, col)

    def intra(k, key, value):
        return pl.pallas_call(
            intra_kernel,
            out_shape=(shape((rows, group_width), BF16), shape((rows, group_width), F32)),
            grid=(1,),
            in_specs=[
                SMEM,
                VMEM,
                VMEM,
                pl.BlockSpec((2 * half, group_width), lambda i: (0, k)),
                pl.BlockSpec((rows, HEAD), lambda i: (0, k)),
                pl.BlockSpec((rows, HEAD), lambda i: (0, k)),
                VMEM,
                VMEM,
            ],
            out_specs=(VMEM, VMEM),
            compiler_params=params(24),
            name=f"intra_{k}",
        )(core, own, other, wq, key, value, col, row)

    held = None
    queries, intras = [], []
    for step, bits in enumerate(ROUNDS):
        final = step == len(ROUNDS) - 1
        got = [lax.ppermute(message, "seq", [(i, i ^ b) for i in range(count)]) for b in bits]
        if step == 0:
            wq = pl.pallas_call(
                stage_kernel,
                out_shape=shape(q_weight.shape, BF16),
                in_specs=[VMEM, HBM],
                out_specs=VMEM,
                scratch_shapes=[pltpu.SemaphoreType.DMA((STAGE_COPIES,))],
                compiler_params=params(2),
                name="stage",
            )(message, in_hbm(q_weight))
        if step in INTRA_STEPS:
            (key, value), _ = lax.optimization_barrier(((key, value), message))
            query, part = intra(INTRA_STEPS.index(step), key, value)
            queries.append(query)
            intras.append(part)
        if final:
            break
        extra = () if held is None else (held,)
        message, held = pl.pallas_call(
            lambda *refs, bits=bits, has=held is not None: combine_kernel(bits, has, *refs),
            out_shape=(shape(message.shape, BF16), shape((state_rows, HEAD), F32)),
            in_specs=[SMEM] + [VMEM] * (2 + len(bits) + len(extra)),
            out_specs=(VMEM, VMEM),
            compiler_params=params(4),
            name="combine",
        )(place, col, message, *got, *extra)
        if step == 0:
            message, wq = lax.optimization_barrier((message, wq))
        if step in INTRA_STEPS:
            message, queries[-1] = lax.optimization_barrier((message, queries[-1]))

    normed, *theirs = pl.pallas_call(
        lambda *refs: norm_kernel(ROUNDS[-1], kv_heads, *refs),
        out_shape=(shape((rows, q_width), BF16),) + (shape((BLOCK, half), BF16),) * (rows // BLOCK),
        in_specs=[SMEM, SMEM] + [VMEM] * (1 + len(got) + 2 * kv_heads + 3),
        out_specs=(VMEM,) * (1 + rows // BLOCK),
        compiler_params=params(16),
        name="norm",
    )(core, place, held, *got, *queries, *intras, col, gain, out_weight)
    received = [swap_head(part) for part in theirs]
    mine = pl.pallas_call(
        own_kernel,
        out_shape=shape((rows, half), F32),
        in_specs=[SMEM, VMEM, VMEM],
        out_specs=VMEM,
        compiler_params=params(16),
        name="own",
    )(core, normed, out_weight)
    out = ()
    for part in range(rows // BLOCK):
        out = (
            pl.pallas_call(
                add_kernel,
                grid=(ADD_STEPS,),
                out_shape=shape((rows, half), BF16),
                in_specs=[VMEM, VMEM] + [HBM] * len(out),
                out_specs=pl.BlockSpec(
                    (BLOCK // ADD_STEPS, half), lambda i, part=part: (i + part * ADD_STEPS, 0)
                ),
                input_output_aliases={2: 0} if out else {},
                compiler_params=params(8),
                name=f"add_{part}",
            )(mine, received[part], *out),
        )
    return out[0]


def solution(mesh):
    return jax.shard_map(
        on_device,
        mesh=mesh,
        in_specs=(
            P("seq", "head"),
            P(None, "head"),
            P(None, "head"),
            P(None, "head"),
            P("head"),
            P("head", None),
            P("seq"),
        ),
        out_specs=P("seq", "head"),
        check_vma=False,
    )
```

```python
import jax
import jax.numpy as jnp
from jax import lax
from jax.experimental import pallas as pl
from jax.experimental.pallas import tpu as pltpu
from jax.sharding import PartitionSpec as P

HEAD = 128
ID_ROWS = 16
BLOCK = 256
ROUNDS = ((1, 2, 3), (6,), (8, 24, 16), (32, 96, 64))
INTRA_STEPS = (1, 2)
CHUNKS = 2
STAGE_COPIES = 4
ADD_STEPS = 2
EPSILON = 1e-05
F32 = jnp.float32
BF16 = jnp.bfloat16

SMEM = pl.BlockSpec(memory_space=pltpu.SMEM)
VMEM = pl.BlockSpec(memory_space=pltpu.VMEM)
HBM = pl.BlockSpec(memory_space=pltpu.HBM)


def params(mib):
    return pltpu.CompilerParams(vmem_limit_bytes=mib << 20)


def dot(a, b):
    return jnp.dot(a, b, preferred_element_type=F32)


def features(x):
    return jnp.where(x > 0.0, x + 1.0, jnp.exp(jnp.minimum(x, 0.0)))


def project(core_ref, own_ref, other_ref, weight_ref):
    half = own_ref.shape[1]
    mine = pl.multiple_of(core_ref[0] * half, half)
    theirs = pl.multiple_of((1 - core_ref[0]) * half, half)
    return dot(own_ref[...], weight_ref[pl.ds(mine, half), :]) + dot(
        other_ref[...], weight_ref[pl.ds(theirs, half), :]
    )


def own_half_kernel(core_ref, ids_hbm, own_hbm, wk_hbm, wv_hbm, *refs):
    own_ref, wk_ref, wv_ref, k_ref, v_ref, col_ref, row_ref, ids_vmem, sems = refs
    half = own_hbm.shape[1]
    chunk = half // CHUNKS
    near = core_ref[0] * half
    far = pl.multiple_of((1 - core_ref[0]) * half, half)
    copies = []
    for c in range(CHUNKS):
        cut = pl.ds(pl.multiple_of(near + c * chunk, chunk), chunk)
        copies.append((own_hbm.at[:, c * chunk : (c + 1) * chunk], own_ref.at[:, c * chunk : (c + 1) * chunk]))
        copies.append((wk_hbm.at[cut, :], wk_ref.at[cut, :]))
        copies.append((wv_hbm.at[cut, :], wv_ref.at[cut, :]))
    cut = pl.ds(far, half)
    copies.append((wk_hbm.at[cut, :], wk_ref.at[cut, :]))
    copies.append((wv_hbm.at[cut, :], wv_ref.at[cut, :]))
    copies.insert(0, (ids_hbm, ids_vmem))
    copies = [pltpu.make_async_copy(a, b, sems.at[i]) for i, (a, b) in enumerate(copies)]
    for copy in copies:
        copy.start()
    copies[0].wait()
    ids = ids_vmem[...].astype(F32)
    row_ref[...] = jnp.broadcast_to(ids, row_ref.shape)
    col_ref[...] = jnp.broadcast_to(ids, (HEAD, ids.shape[1])).T
    for c in range(CHUNKS):
        for copy in copies[3 * c + 1 : 3 * c + 4]:
            copy.wait()
        own = own_ref[:, c * chunk : (c + 1) * chunk]
        cut = pl.ds(pl.multiple_of(near + c * chunk, chunk), chunk)
        key = dot(own, wk_ref[cut, :])
        value = dot(own, wv_ref[cut, :])
        if c == 0:
            k_ref[...] = key
            v_ref[...] = value
        else:
            k_ref[...] += key
            v_ref[...] += value
    for copy in copies[3 * CHUNKS + 1 :]:
        copy.wait()


def key_value_kernel(core_ref, other_ref, k_part_ref, v_part_ref, wk_ref, wv_ref, col_ref, *outs):
    k_ref, v_ref, message_ref = outs
    rows, half = other_ref.shape
    other = other_ref[...]
    far = pl.ds(pl.multiple_of((1 - core_ref[0]) * half, half), half)
    key = features(k_part_ref[...] + dot(other, wk_ref[far, :])).astype(BF16)
    value = (v_part_ref[...] + dot(other, wv_ref[far, :])).astype(BF16)
    k_ref[...] = key
    v_ref[...] = value
    last = col_ref[rows - 1 : rows, :]
    tail = col_ref[...] == last
    heads = key.shape[1] // HEAD
    for h in range(heads):
        cut = slice(h * HEAD, (h + 1) * HEAD)
        tail_key = jnp.where(tail, key[:, cut].astype(F32), 0.0).astype(BF16)
        state = lax.dot_general(
            tail_key, value[:, cut], (((0,), (0,)), ((), ())), preferred_element_type=F32
        )
        message_ref[cut, :] = state.astype(BF16)
    message_ref[heads * HEAD :, :] = jnp.broadcast_to(last, (ID_ROWS, HEAD)).astype(BF16)


def stage_kernel(after_ref, weight_hbm, weight_ref, sems):
    size = weight_ref.shape[0] // STAGE_COPIES
    copies = []
    for i in range(STAGE_COPIES):
        cut = slice(i * size, (i + 1) * size)
        copies.append(pltpu.make_async_copy(weight_hbm.at[cut, :], weight_ref.at[cut, :], sems.at[i]))
    for copy in copies:
        copy.start()
    for copy in copies:
        copy.wait()


def intra_kernel(core_ref, own_ref, other_ref, wq_ref, k_ref, v_ref, col_ref, row_ref, q_ref, intra_ref):
    rows = own_ref.shape[0]
    group = wq_ref.shape[1] // HEAD
    q_ref[...] = features(project(core_ref, own_ref, other_ref, wq_ref)).astype(BF16)
    for start in range(0, rows, BLOCK):
        seen = start + BLOCK
        here = slice(start, seen)
        key = k_ref[:seen, :]
        value = v_ref[:seen, :]
        t = lax.broadcasted_iota(jnp.int32, (BLOCK, seen), 0) + start
        s = lax.broadcasted_iota(jnp.int32, (BLOCK, seen), 1)
        same = (col_ref[here, :1] == row_ref[:1, :seen]) & (t >= s)
        for g in range(group):
            cut = slice(g * HEAD, (g + 1) * HEAD)
            scores = lax.dot_general(
                q_ref[here, cut], key, (((1,), (1,)), ((), ())), preferred_element_type=F32
            )
            scores = jnp.where(same, scores, 0.0).astype(BF16)
            intra_ref[here, cut] = dot(scores, value)


def combine_kernel(bits, has_held, place_ref, col_ref, message_ref, *refs):
    got = refs[: len(bits)]
    held_in = refs[len(bits)] if has_held else None
    next_ref, held_ref = refs[-2:]
    rows = message_ref.shape[0] - ID_ROWS
    own_id = message_ref[rows : rows + 1, :].astype(F32)
    ids = [g[rows : rows + 1, :].astype(F32) for g in got]
    top = own_id
    for i in ids:
        top = jnp.maximum(top, i)
    first = col_ref[:1, :]
    total = jnp.where(own_id == top, message_ref[:rows, :].astype(F32), 0.0)
    held = held_in[...] if has_held else jnp.zeros((rows, HEAD), F32)
    for b, g, i in zip(bits, got, ids):
        state = g[:rows, :].astype(F32)
        earlier = (place_ref[0] & (1 << (b.bit_length() - 1))) != 0
        held = held + jnp.where((i == first) & earlier, state, 0.0)
        total = total + jnp.where(i == top, state, 0.0)
    next_ref[:rows, :] = total.astype(BF16)
    next_ref[rows:, :] = jnp.broadcast_to(top, (ID_ROWS, HEAD)).astype(BF16)
    held_ref[...] = held


def incoming_of(bits, place_ref, col_ref, held_ref, got):
    first = col_ref[:1, :]
    rows = held_ref.shape[0]
    held = held_ref[...]
    for b, g in zip(bits, got):
        earlier = (place_ref[0] & (1 << (b.bit_length() - 1))) != 0
        same = (g[rows : rows + 1, :].astype(F32) == first) & earlier
        held = held + jnp.where(same, g[:rows, :].astype(F32), 0.0)
    return held.astype(BF16)


def norm_kernel(bits, groups, core_ref, place_ref, held_ref, *refs):
    got, refs = refs[: len(bits)], refs[len(bits) :]
    queries, intras, refs = refs[:groups], refs[groups : 2 * groups], refs[2 * groups :]
    col_ref, gain_ref, weight_ref, normed_ref, *theirs = refs
    incoming = incoming_of(bits, place_ref, col_ref, held_ref, got)
    for start in range(0, col_ref.shape[0], BLOCK):
        here = slice(start, start + BLOCK)
        joins = col_ref[here, :] == col_ref[:1, :]
        for k in range(groups):
            width = queries[k].shape[1]
            for g in range(width // HEAD):
                cut = slice(g * HEAD, (g + 1) * HEAD)
                out = slice(k * width + g * HEAD, k * width + (g + 1) * HEAD)
                carried = dot(queries[k][here, cut], incoming[k * HEAD : (k + 1) * HEAD, :])
                combined = intras[k][here, cut] + jnp.where(joins, carried, 0.0)
                scale = lax.rsqrt(jnp.mean(combined * combined, axis=-1, keepdims=True) + EPSILON)
                normed_ref[here, out] = (combined * scale * gain_ref[:1, out]).astype(BF16)
        theirs[start // BLOCK][...] = dot(normed_ref[here, :], columns(weight_ref, 1 - core_ref[0])).astype(BF16)


def columns(weight_ref, part):
    half = weight_ref.shape[1] // 2
    return weight_ref[:, pl.ds(pl.multiple_of(part * half, half), half)]


def own_kernel(core_ref, normed_ref, weight_ref, out_ref):
    out_ref[...] = dot(normed_ref[...], columns(weight_ref, core_ref[0]))


def add_kernel(mine_ref, theirs_ref, *refs):
    out_ref = refs[-1]
    size = out_ref.shape[0]
    step = pl.program_id(0)
    first = pl.multiple_of((step + (pl.num_programs(0) if len(refs) > 1 else 0)) * size, size)
    here = pl.ds(pl.multiple_of(step * size, size), size)
    out_ref[...] = (mine_ref[pl.ds(first, size), :] + theirs_ref[here, :].astype(F32)).astype(BF16)


def shape(dims, dtype):
    return jax.ShapeDtypeStruct(dims, dtype)


def in_hbm(x):
    return pltpu.with_memory_space_constraint(x, pltpu.HBM)


def swap_head(x):
    return lax.ppermute(x, "head", [(0, 1), (1, 0)])


def on_device(tokens, q_weight, key_matrix, value_matrix, norm_gain, out_weight, doc_ids):
    rows, half = tokens.shape
    kv_width = key_matrix.shape[1]
    q_width = q_weight.shape[1]
    kv_heads = kv_width // HEAD
    group_width = q_width // kv_heads
    state_rows = kv_heads * HEAD
    count = lax.axis_size("seq")
    core = lax.axis_index("head").astype(jnp.int32).reshape(1)
    place = lax.axis_index("seq").astype(jnp.int32).reshape(1)
    other = swap_head(tokens)
    gain = norm_gain.reshape(1, q_width)
    own, wk, wv, k_part, v_part, col, row = pl.pallas_call(
        own_half_kernel,
        out_shape=(
            shape(tokens.shape, BF16),
            shape(key_matrix.shape, BF16),
            shape(value_matrix.shape, BF16),
            shape((rows, kv_width), F32),
            shape((rows, kv_width), F32),
            shape((rows, HEAD), F32),
            shape((8, rows), F32),
        ),
        in_specs=[SMEM, HBM, HBM, HBM, HBM],
        out_specs=(VMEM,) * 7,
        scratch_shapes=[pltpu.VMEM((1, rows), jnp.int32), pltpu.SemaphoreType.DMA((3 * CHUNKS + 3,))],
        compiler_params=params(8),
        name="own_half",
    )(core, *(in_hbm(x) for x in (doc_ids.reshape(1, rows), tokens, key_matrix, value_matrix)))

    key, value, message = pl.pallas_call(
        key_value_kernel,
        out_shape=(
            shape((rows, kv_width), BF16),
            shape((rows, kv_width), BF16),
            shape((state_rows + ID_ROWS, HEAD), BF16),
        ),
        in_specs=[SMEM] + [VMEM] * 6,
        out_specs=(VMEM, VMEM, VMEM),
        compiler_params=params(16),
        name="key_value",
    )(core, other, k_part, v_part, wk, wv, col)

    def intra(k, key, value):
        return pl.pallas_call(
            intra_kernel,
            out_shape=(shape((rows, group_width), BF16), shape((rows, group_width), F32)),
            grid=(1,),
            in_specs=[
                SMEM,
                VMEM,
                VMEM,
                pl.BlockSpec((2 * half, group_width), lambda i: (0, k)),
                pl.BlockSpec((rows, HEAD), lambda i: (0, k)),
                pl.BlockSpec((rows, HEAD), lambda i: (0, k)),
                VMEM,
                VMEM,
            ],
            out_specs=(VMEM, VMEM),
            compiler_params=params(24),
            name=f"intra_{k}",
        )(core, own, other, wq, key, value, col, row)

    held = None
    queries, intras = [], []
    for step, bits in enumerate(ROUNDS):
        final = step == len(ROUNDS) - 1
        got = [lax.ppermute(message, "seq", [(i, i ^ b) for i in range(count)]) for b in bits]
        if step == 0:
            wq = pl.pallas_call(
                stage_kernel,
                out_shape=shape(q_weight.shape, BF16),
                in_specs=[VMEM, HBM],
                out_specs=VMEM,
                scratch_shapes=[pltpu.SemaphoreType.DMA((STAGE_COPIES,))],
                compiler_params=params(2),
                name="stage",
            )(message, in_hbm(q_weight))
        if step in INTRA_STEPS:
            (key, value), _ = lax.optimization_barrier(((key, value), message))
            query, part = intra(INTRA_STEPS.index(step), key, value)
            queries.append(query)
            intras.append(part)
        if final:
            break
        extra = () if held is None else (held,)
        message, held = pl.pallas_call(
            lambda *refs, bits=bits, has=held is not None: combine_kernel(bits, has, *refs),
            out_shape=(shape(message.shape, BF16), shape((state_rows, HEAD), F32)),
            in_specs=[SMEM] + [VMEM] * (2 + len(bits) + len(extra)),
            out_specs=(VMEM, VMEM),
            compiler_params=params(4),
            name="combine",
        )(place, col, message, *got, *extra)
        if step == 0:
            message, wq = lax.optimization_barrier((message, wq))
        if step in INTRA_STEPS:
            message, queries[-1] = lax.optimization_barrier((message, queries[-1]))

    normed, *theirs = pl.pallas_call(
        lambda *refs: norm_kernel(ROUNDS[-1], kv_heads, *refs),
        out_shape=(shape((rows, q_width), BF16),) + (shape((BLOCK, half), BF16),) * (rows // BLOCK),
        in_specs=[SMEM, SMEM] + [VMEM] * (1 + len(got) + 2 * kv_heads + 3),
        out_specs=(VMEM,) * (1 + rows // BLOCK),
        compiler_params=params(16),
        name="norm",
    )(core, place, held, *got, *queries, *intras, col, gain, out_weight)
    received = [swap_head(part) for part in theirs]
    mine = pl.pallas_call(
        own_kernel,
        out_shape=shape((rows, half), F32),
        in_specs=[SMEM, VMEM, VMEM],
        out_specs=VMEM,
        compiler_params=params(16),
        name="own",
    )(core, normed, out_weight)
    out = ()
    for part in range(rows // BLOCK):
        out = (
            pl.pallas_call(
                add_kernel,
                grid=(ADD_STEPS,),
                out_shape=shape((rows, half), BF16),
                in_specs=[VMEM, VMEM] + [HBM] * len(out),
                out_specs=pl.BlockSpec(
                    (BLOCK // ADD_STEPS, half), lambda i, part=part: (i + part * ADD_STEPS, 0)
                ),
                input_output_aliases={2: 0} if out else {},
                compiler_params=params(8),
                name=f"add_{part}",
            )(mine, received[part], *out),
        )
    return out[0]


def solution(mesh):
    return jax.shard_map(
        on_device,
        mesh=mesh,
        in_specs=(
            P("seq", "head"),
            P(None, "head"),
            P(None, "head"),
            P(None, "head"),
            P("head"),
            P("head", None),
            P("seq"),
        ),
        out_specs=P("seq", "head"),
        check_vma=False,
    )
```

```python
import jax
import jax.numpy as jnp
from jax import lax
from jax.experimental import pallas as pl
from jax.experimental.pallas import tpu as pltpu
from jax.sharding import PartitionSpec as P

HEAD = 128
ID_ROWS = 16
BLOCK = 256
ROUNDS = ((1, 2, 3), (6,), (8, 24, 16), (32, 96, 64))
INTRA_STEPS = (1, 2)
CHUNKS = 2
STAGE_COPIES = 4
ADD_STEPS = 2
EPSILON = 1e-05
F32 = jnp.float32
BF16 = jnp.bfloat16

SMEM = pl.BlockSpec(memory_space=pltpu.SMEM)
VMEM = pl.BlockSpec(memory_space=pltpu.VMEM)
HBM = pl.BlockSpec(memory_space=pltpu.HBM)


def params(mib):
    return pltpu.CompilerParams(vmem_limit_bytes=mib << 20)


def dot(a, b):
    return jnp.dot(a, b, preferred_element_type=F32)


def features(x):
    return jnp.where(x > 0.0, x + 1.0, jnp.exp(jnp.minimum(x, 0.0)))


def project(core_ref, own_ref, other_ref, weight_ref):
    half = own_ref.shape[1]
    mine = pl.multiple_of(core_ref[0] * half, half)
    theirs = pl.multiple_of((1 - core_ref[0]) * half, half)
    return dot(own_ref[...], weight_ref[pl.ds(mine, half), :]) + dot(
        other_ref[...], weight_ref[pl.ds(theirs, half), :]
    )


def own_half_kernel(core_ref, ids_hbm, own_hbm, wk_hbm, wv_hbm, *refs):
    own_ref, wk_ref, wv_ref, k_ref, v_ref, col_ref, row_ref, ids_vmem, sems = refs
    half = own_hbm.shape[1]
    chunk = half // CHUNKS
    near = core_ref[0] * half
    far = pl.multiple_of((1 - core_ref[0]) * half, half)
    copies = []
    for c in range(CHUNKS):
        cut = pl.ds(pl.multiple_of(near + c * chunk, chunk), chunk)
        copies.append((own_hbm.at[:, c * chunk : (c + 1) * chunk], own_ref.at[:, c * chunk : (c + 1) * chunk]))
        copies.append((wk_hbm.at[cut, :], wk_ref.at[cut, :]))
        copies.append((wv_hbm.at[cut, :], wv_ref.at[cut, :]))
    cut = pl.ds(far, half)
    copies.append((wk_hbm.at[cut, :], wk_ref.at[cut, :]))
    copies.append((wv_hbm.at[cut, :], wv_ref.at[cut, :]))
    copies.insert(0, (ids_hbm, ids_vmem))
    copies = [pltpu.make_async_copy(a, b, sems.at[i]) for i, (a, b) in enumerate(copies)]
    for copy in copies:
        copy.start()
    copies[0].wait()
    ids = ids_vmem[...].astype(F32)
    row_ref[...] = jnp.broadcast_to(ids, row_ref.shape)
    col_ref[...] = jnp.broadcast_to(ids, (HEAD, ids.shape[1])).T
    for c in range(CHUNKS):
        for copy in copies[3 * c + 1 : 3 * c + 4]:
            copy.wait()
        own = own_ref[:, c * chunk : (c + 1) * chunk]
        cut = pl.ds(pl.multiple_of(near + c * chunk, chunk), chunk)
        key = dot(own, wk_ref[cut, :])
        value = dot(own, wv_ref[cut, :])
        if c == 0:
            k_ref[...] = key
            v_ref[...] = value
        else:
            k_ref[...] += key
            v_ref[...] += value
    for copy in copies[3 * CHUNKS + 1 :]:
        copy.wait()


def key_value_kernel(core_ref, other_ref, k_part_ref, v_part_ref, wk_ref, wv_ref, col_ref, *outs):
    k_ref, v_ref, message_ref = outs
    rows, half = other_ref.shape
    other = other_ref[...]
    far = pl.ds(pl.multiple_of((1 - core_ref[0]) * half, half), half)
    key = features(k_part_ref[...] + dot(other, wk_ref[far, :])).astype(BF16)
    value = (v_part_ref[...] + dot(other, wv_ref[far, :])).astype(BF16)
    k_ref[...] = key
    v_ref[...] = value
    last = col_ref[rows - 1 : rows, :]
    tail = col_ref[...] == last
    heads = key.shape[1] // HEAD
    for h in range(heads):
        cut = slice(h * HEAD, (h + 1) * HEAD)
        tail_key = jnp.where(tail, key[:, cut].astype(F32), 0.0).astype(BF16)
        state = lax.dot_general(
            tail_key, value[:, cut], (((0,), (0,)), ((), ())), preferred_element_type=F32
        )
        message_ref[cut, :] = state.astype(BF16)
    message_ref[heads * HEAD :, :] = jnp.broadcast_to(last, (ID_ROWS, HEAD)).astype(BF16)


def stage_kernel(core_ref, after_ref, wq_hbm, out_hbm, wq_ref, far_ref, sems):
    half = far_ref.shape[1]
    far = pl.ds(pl.multiple_of((1 - core_ref[0]) * half, half), half)
    copies = []
    for i in range(STAGE_COPIES):
        size = wq_ref.shape[0] // STAGE_COPIES
        cut = slice(i * size, (i + 1) * size)
        copies.append((wq_hbm.at[cut, :], wq_ref.at[cut, :]))
        size = far_ref.shape[0] // STAGE_COPIES
        cut = slice(i * size, (i + 1) * size)
        copies.append((out_hbm.at[cut, far], far_ref.at[cut, :]))
    copies = [pltpu.make_async_copy(a, b, sems.at[i]) for i, (a, b) in enumerate(copies)]
    for copy in copies:
        copy.start()
    for copy in copies:
        copy.wait()


def intra_kernel(core_ref, own_ref, other_ref, wq_ref, k_ref, v_ref, col_ref, row_ref, q_ref, intra_ref):
    rows = own_ref.shape[0]
    group = wq_ref.shape[1] // HEAD
    q_ref[...] = features(project(core_ref, own_ref, other_ref, wq_ref)).astype(BF16)
    for start in range(0, rows, BLOCK):
        seen = start + BLOCK
        here = slice(start, seen)
        key = k_ref[:seen, :]
        value = v_ref[:seen, :]
        t = lax.broadcasted_iota(jnp.int32, (BLOCK, seen), 0) + start
        s = lax.broadcasted_iota(jnp.int32, (BLOCK, seen), 1)
        same = (col_ref[here, :1] == row_ref[:1, :seen]) & (t >= s)
        for g in range(group):
            cut = slice(g * HEAD, (g + 1) * HEAD)
            scores = lax.dot_general(
                q_ref[here, cut], key, (((1,), (1,)), ((), ())), preferred_element_type=F32
            )
            scores = jnp.where(same, scores, 0.0).astype(BF16)
            intra_ref[here, cut] = dot(scores, value)


def combine_kernel(bits, has_held, place_ref, col_ref, message_ref, *refs):
    got = refs[: len(bits)]
    held_in = refs[len(bits)] if has_held else None
    next_ref, held_ref = refs[-2:]
    rows = message_ref.shape[0] - ID_ROWS
    own_id = message_ref[rows : rows + 1, :].astype(F32)
    ids = [g[rows : rows + 1, :].astype(F32) for g in got]
    top = own_id
    for i in ids:
        top = jnp.maximum(top, i)
    first = col_ref[:1, :]
    total = jnp.where(own_id == top, message_ref[:rows, :].astype(F32), 0.0)
    held = held_in[...] if has_held else jnp.zeros((rows, HEAD), F32)
    for b, g, i in zip(bits, got, ids):
        state = g[:rows, :].astype(F32)
        earlier = (place_ref[0] & (1 << (b.bit_length() - 1))) != 0
        held = held + jnp.where((i == first) & earlier, state, 0.0)
        total = total + jnp.where(i == top, state, 0.0)
    next_ref[:rows, :] = total.astype(BF16)
    next_ref[rows:, :] = jnp.broadcast_to(top, (ID_ROWS, HEAD)).astype(BF16)
    held_ref[...] = held


def incoming_of(bits, place_ref, col_ref, held_ref, got):
    first = col_ref[:1, :]
    rows = held_ref.shape[0]
    held = held_ref[...]
    for b, g in zip(bits, got):
        earlier = (place_ref[0] & (1 << (b.bit_length() - 1))) != 0
        same = (g[rows : rows + 1, :].astype(F32) == first) & earlier
        held = held + jnp.where(same, g[:rows, :].astype(F32), 0.0)
    return held.astype(BF16)


def norm_kernel(bits, groups, place_ref, held_ref, *refs):
    got, refs = refs[: len(bits)], refs[len(bits) :]
    queries, intras, refs = refs[:groups], refs[groups : 2 * groups], refs[2 * groups :]
    col_ref, gain_ref, *normed = refs
    incoming = incoming_of(bits, place_ref, col_ref, held_ref, got)
    for start in range(0, col_ref.shape[0], BLOCK):
        here = slice(start, start + BLOCK)
        joins = col_ref[here, :] == col_ref[:1, :]
        for k in range(groups):
            width = queries[k].shape[1]
            for g in range(width // HEAD):
                cut = slice(g * HEAD, (g + 1) * HEAD)
                out = slice(k * width + g * HEAD, k * width + (g + 1) * HEAD)
                carried = dot(queries[k][here, cut], incoming[k * HEAD : (k + 1) * HEAD, :])
                combined = intras[k][here, cut] + jnp.where(joins, carried, 0.0)
                scale = lax.rsqrt(jnp.mean(combined * combined, axis=-1, keepdims=True) + EPSILON)
                normed[start // BLOCK][:, out] = (combined * scale * gain_ref[:1, out]).astype(BF16)


def columns(weight_ref, part):
    half = weight_ref.shape[1] // 2
    return weight_ref[:, pl.ds(pl.multiple_of(part * half, half), half)]


def own_kernel(core_ref, *refs):
    *normed, weight_ref, out_ref = refs
    weight = columns(weight_ref, core_ref[0])
    out_ref[...] = dot(jnp.concatenate([part[...] for part in normed]), weight)


def add_kernel(mine_ref, other_ref, near_ref, *refs):
    out_ref = refs[-1]
    width = out_ref.shape[1]
    cut = pl.ds(pl.multiple_of(pl.program_id(0) * width, width), width)
    rows = other_ref.shape[0]
    first = mine_ref.shape[0] - rows if len(refs) > 1 else 0
    product = dot(other_ref[...], near_ref[:, cut])
    out_ref[...] = (mine_ref[first : first + rows, cut] + product).astype(BF16)


def shape(dims, dtype):
    return jax.ShapeDtypeStruct(dims, dtype)


def in_hbm(x):
    return pltpu.with_memory_space_constraint(x, pltpu.HBM)


def swap_head(x):
    return lax.ppermute(x, "head", [(0, 1), (1, 0)])


def on_device(tokens, q_weight, key_matrix, value_matrix, norm_gain, out_weight, doc_ids):
    rows, half = tokens.shape
    kv_width = key_matrix.shape[1]
    q_width = q_weight.shape[1]
    kv_heads = kv_width // HEAD
    group_width = q_width // kv_heads
    state_rows = kv_heads * HEAD
    count = lax.axis_size("seq")
    core = lax.axis_index("head").astype(jnp.int32).reshape(1)
    place = lax.axis_index("seq").astype(jnp.int32).reshape(1)
    other = swap_head(tokens)
    gain = norm_gain.reshape(1, q_width)
    own, wk, wv, k_part, v_part, col, row = pl.pallas_call(
        own_half_kernel,
        out_shape=(
            shape(tokens.shape, BF16),
            shape(key_matrix.shape, BF16),
            shape(value_matrix.shape, BF16),
            shape((rows, kv_width), F32),
            shape((rows, kv_width), F32),
            shape((rows, HEAD), F32),
            shape((8, rows), F32),
        ),
        in_specs=[SMEM, HBM, HBM, HBM, HBM],
        out_specs=(VMEM,) * 7,
        scratch_shapes=[pltpu.VMEM((1, rows), jnp.int32), pltpu.SemaphoreType.DMA((3 * CHUNKS + 3,))],
        compiler_params=params(8),
        name="own_half",
    )(core, *(in_hbm(x) for x in (doc_ids.reshape(1, rows), tokens, key_matrix, value_matrix)))

    key, value, message = pl.pallas_call(
        key_value_kernel,
        out_shape=(
            shape((rows, kv_width), BF16),
            shape((rows, kv_width), BF16),
            shape((state_rows + ID_ROWS, HEAD), BF16),
        ),
        in_specs=[SMEM] + [VMEM] * 6,
        out_specs=(VMEM, VMEM, VMEM),
        compiler_params=params(16),
        name="key_value",
    )(core, other, k_part, v_part, wk, wv, col)

    def intra(k, key, value):
        return pl.pallas_call(
            intra_kernel,
            out_shape=(shape((rows, group_width), BF16), shape((rows, group_width), F32)),
            grid=(1,),
            in_specs=[
                SMEM,
                VMEM,
                VMEM,
                pl.BlockSpec((2 * half, group_width), lambda i: (0, k)),
                pl.BlockSpec((rows, HEAD), lambda i: (0, k)),
                pl.BlockSpec((rows, HEAD), lambda i: (0, k)),
                VMEM,
                VMEM,
            ],
            out_specs=(VMEM, VMEM),
            compiler_params=params(24),
            name=f"intra_{k}",
        )(core, own, other, wq, key, value, col, row)

    held = None
    queries, intras = [], []
    for step, bits in enumerate(ROUNDS):
        final = step == len(ROUNDS) - 1
        got = [lax.ppermute(message, "seq", [(i, i ^ b) for i in range(count)]) for b in bits]
        if step == 0:
            wq, far = pl.pallas_call(
                stage_kernel,
                out_shape=(shape(q_weight.shape, BF16), shape((q_width, half), BF16)),
                in_specs=[SMEM, VMEM, HBM, HBM],
                out_specs=(VMEM, VMEM),
                scratch_shapes=[pltpu.SemaphoreType.DMA((2 * STAGE_COPIES,))],
                compiler_params=params(2),
                name="stage",
            )(core, message, in_hbm(q_weight), in_hbm(out_weight))
        if step in INTRA_STEPS:
            (key, value), _ = lax.optimization_barrier(((key, value), message))
            query, part = intra(INTRA_STEPS.index(step), key, value)
            queries.append(query)
            intras.append(part)
        if final:
            break
        extra = () if held is None else (held,)
        message, held = pl.pallas_call(
            lambda *refs, bits=bits, has=held is not None: combine_kernel(bits, has, *refs),
            out_shape=(shape(message.shape, BF16), shape((state_rows, HEAD), F32)),
            in_specs=[SMEM] + [VMEM] * (2 + len(bits) + len(extra)),
            out_specs=(VMEM, VMEM),
            compiler_params=params(4),
            name="combine",
        )(place, col, message, *got, *extra)
        if step == 0:
            message, wq, far = lax.optimization_barrier((message, wq, far))
            near = swap_head(far)
        if step in INTRA_STEPS:
            message, queries[-1] = lax.optimization_barrier((message, queries[-1]))

    parts = rows // BLOCK
    normed = pl.pallas_call(
        lambda *refs: norm_kernel(ROUNDS[-1], kv_heads, *refs),
        out_shape=(shape((BLOCK, q_width), BF16),) * parts,
        in_specs=[SMEM] + [VMEM] * (1 + len(got) + 2 * kv_heads + 2),
        out_specs=(VMEM,) * parts,
        compiler_params=params(16),
        name="norm",
    )(place, held, *got, *queries, *intras, col, gain)
    received = [swap_head(part) for part in normed]
    mine = pl.pallas_call(
        own_kernel,
        out_shape=shape((rows, half), F32),
        in_specs=[SMEM] + [VMEM] * (parts + 1),
        out_specs=VMEM,
        compiler_params=params(16),
        name="own",
    )(core, *normed, out_weight)
    out = ()
    for part in range(parts):
        out = (
            pl.pallas_call(
                add_kernel,
                grid=(ADD_STEPS,),
                out_shape=shape((rows, half), BF16),
                in_specs=[VMEM, VMEM, VMEM] + [HBM] * len(out),
                out_specs=pl.BlockSpec((BLOCK, half // ADD_STEPS), lambda i, part=part: (part, i)),
                input_output_aliases={3: 0} if out else {},
                compiler_params=params(8),
                name=f"add_{part}",
            )(mine, received[part], near, *out),
        )
    return out[0]


def solution(mesh):
    return jax.shard_map(
        on_device,
        mesh=mesh,
        in_specs=(
            P("seq", "head"),
            P(None, "head"),
            P(None, "head"),
            P(None, "head"),
            P("head"),
            P("head", None),
            P("seq"),
        ),
        out_specs=P("seq", "head"),
        check_vma=False,
    )
```

```python
import jax
import jax.numpy as jnp
from jax import lax
from jax.experimental import pallas as pl
from jax.experimental.pallas import tpu as pltpu
from jax.sharding import PartitionSpec as P

HEAD = 128
ID_ROWS = 16
BLOCK = 256
NORM_BLOCK = 512
ROUNDS = ((1, 2, 3), (6,), (8, 24, 16), (32, 96, 64))
INTRA_STEPS = (1, 2)
CHUNKS = 2
STAGE_COPIES = 4
ADD_STEPS = 2
EPSILON = 1e-05
F32 = jnp.float32
BF16 = jnp.bfloat16

SMEM = pl.BlockSpec(memory_space=pltpu.SMEM)
VMEM = pl.BlockSpec(memory_space=pltpu.VMEM)
HBM = pl.BlockSpec(memory_space=pltpu.HBM)


def params(mib):
    return pltpu.CompilerParams(vmem_limit_bytes=mib << 20)


def dot(a, b):
    return jnp.dot(a, b, preferred_element_type=F32)


def features(x):
    return jnp.where(x > 0.0, x + 1.0, jnp.exp(jnp.minimum(x, 0.0)))


def project(core_ref, own_ref, other_ref, weight_ref):
    half = own_ref.shape[1]
    mine = pl.multiple_of(core_ref[0] * half, half)
    theirs = pl.multiple_of((1 - core_ref[0]) * half, half)
    return dot(own_ref[...], weight_ref[pl.ds(mine, half), :]) + dot(
        other_ref[...], weight_ref[pl.ds(theirs, half), :]
    )


def own_half_kernel(core_ref, ids_hbm, own_hbm, wk_hbm, wv_hbm, *refs):
    own_ref, wk_ref, wv_ref, k_ref, v_ref, col_ref, row_ref, ids_vmem, sems = refs
    half = own_hbm.shape[1]
    chunk = half // CHUNKS
    near = core_ref[0] * half
    far = pl.multiple_of((1 - core_ref[0]) * half, half)
    copies = []
    for c in range(CHUNKS):
        cut = pl.ds(pl.multiple_of(near + c * chunk, chunk), chunk)
        copies.append((own_hbm.at[:, c * chunk : (c + 1) * chunk], own_ref.at[:, c * chunk : (c + 1) * chunk]))
        copies.append((wk_hbm.at[cut, :], wk_ref.at[cut, :]))
        copies.append((wv_hbm.at[cut, :], wv_ref.at[cut, :]))
    cut = pl.ds(far, half)
    copies.append((wk_hbm.at[cut, :], wk_ref.at[cut, :]))
    copies.append((wv_hbm.at[cut, :], wv_ref.at[cut, :]))
    copies.insert(0, (ids_hbm, ids_vmem))
    copies = [pltpu.make_async_copy(a, b, sems.at[i]) for i, (a, b) in enumerate(copies)]
    for copy in copies:
        copy.start()
    copies[0].wait()
    ids = ids_vmem[...].astype(F32)
    row_ref[...] = jnp.broadcast_to(ids, row_ref.shape)
    col_ref[...] = jnp.broadcast_to(ids, (HEAD, ids.shape[1])).T
    for c in range(CHUNKS):
        for copy in copies[3 * c + 1 : 3 * c + 4]:
            copy.wait()
        own = own_ref[:, c * chunk : (c + 1) * chunk]
        cut = pl.ds(pl.multiple_of(near + c * chunk, chunk), chunk)
        key = dot(own, wk_ref[cut, :])
        value = dot(own, wv_ref[cut, :])
        if c == 0:
            k_ref[...] = key
            v_ref[...] = value
        else:
            k_ref[...] += key
            v_ref[...] += value
    for copy in copies[3 * CHUNKS + 1 :]:
        copy.wait()


def key_value_kernel(core_ref, other_ref, k_part_ref, v_part_ref, wk_ref, wv_ref, col_ref, *outs):
    k_ref, v_ref, message_ref = outs
    rows, half = other_ref.shape
    other = other_ref[...]
    far = pl.ds(pl.multiple_of((1 - core_ref[0]) * half, half), half)
    key = features(k_part_ref[...] + dot(other, wk_ref[far, :])).astype(BF16)
    value = (v_part_ref[...] + dot(other, wv_ref[far, :])).astype(BF16)
    k_ref[...] = key
    v_ref[...] = value
    last = col_ref[rows - 1 : rows, :]
    tail = col_ref[...] == last
    heads = key.shape[1] // HEAD
    for h in range(heads):
        cut = slice(h * HEAD, (h + 1) * HEAD)
        tail_key = jnp.where(tail, key[:, cut].astype(F32), 0.0).astype(BF16)
        state = lax.dot_general(
            tail_key, value[:, cut], (((0,), (0,)), ((), ())), preferred_element_type=F32
        )
        message_ref[cut, :] = state.astype(BF16)
    message_ref[heads * HEAD :, :] = jnp.broadcast_to(last, (ID_ROWS, HEAD)).astype(BF16)


def stage_kernel(after_ref, weight_hbm, weight_ref, sems):
    size = weight_ref.shape[0] // STAGE_COPIES
    copies = []
    for i in range(STAGE_COPIES):
        cut = slice(i * size, (i + 1) * size)
        copies.append(pltpu.make_async_copy(weight_hbm.at[cut, :], weight_ref.at[cut, :], sems.at[i]))
    for copy in copies:
        copy.start()
    for copy in copies:
        copy.wait()


def intra_kernel(core_ref, own_ref, other_ref, wq_ref, k_ref, v_ref, col_ref, row_ref, q_ref, intra_ref):
    rows = own_ref.shape[0]
    group = wq_ref.shape[1] // HEAD
    q_ref[...] = features(project(core_ref, own_ref, other_ref, wq_ref)).astype(BF16)
    for start in range(0, rows, BLOCK):
        seen = start + BLOCK
        here = slice(start, seen)
        key = k_ref[:seen, :]
        value = v_ref[:seen, :]
        t = lax.broadcasted_iota(jnp.int32, (BLOCK, seen), 0) + start
        s = lax.broadcasted_iota(jnp.int32, (BLOCK, seen), 1)
        same = (col_ref[here, :1] == row_ref[:1, :seen]) & (t >= s)
        for g in range(group):
            cut = slice(g * HEAD, (g + 1) * HEAD)
            scores = lax.dot_general(
                q_ref[here, cut], key, (((1,), (1,)), ((), ())), preferred_element_type=F32
            )
            scores = jnp.where(same, scores, 0.0).astype(BF16)
            intra_ref[here, cut] = dot(scores, value)


def combine_kernel(bits, has_held, place_ref, col_ref, message_ref, *refs):
    got = refs[: len(bits)]
    held_in = refs[len(bits)] if has_held else None
    next_ref, held_ref = refs[-2:]
    rows = message_ref.shape[0] - ID_ROWS
    own_id = message_ref[rows : rows + 1, :].astype(F32)
    ids = [g[rows : rows + 1, :].astype(F32) for g in got]
    top = own_id
    for i in ids:
        top = jnp.maximum(top, i)
    first = col_ref[:1, :]
    total = jnp.where(own_id == top, message_ref[:rows, :].astype(F32), 0.0)
    held = held_in[...] if has_held else jnp.zeros((rows, HEAD), F32)
    for b, g, i in zip(bits, got, ids):
        state = g[:rows, :].astype(F32)
        earlier = (place_ref[0] & (1 << (b.bit_length() - 1))) != 0
        held = held + jnp.where((i == first) & earlier, state, 0.0)
        total = total + jnp.where(i == top, state, 0.0)
    next_ref[:rows, :] = total.astype(BF16)
    next_ref[rows:, :] = jnp.broadcast_to(top, (ID_ROWS, HEAD)).astype(BF16)
    held_ref[...] = held


def incoming_of(bits, place_ref, col_ref, held_ref, got):
    first = col_ref[:1, :]
    rows = held_ref.shape[0]
    held = held_ref[...]
    for b, g in zip(bits, got):
        earlier = (place_ref[0] & (1 << (b.bit_length() - 1))) != 0
        same = (g[rows : rows + 1, :].astype(F32) == first) & earlier
        held = held + jnp.where(same, g[:rows, :].astype(F32), 0.0)
    return held.astype(BF16)


def norm_kernel(bits, groups, core_ref, place_ref, held_ref, *refs):
    got, refs = refs[: len(bits)], refs[len(bits) :]
    queries, intras, refs = refs[:groups], refs[groups : 2 * groups], refs[2 * groups :]
    col_ref, gain_ref, weight_ref, normed_ref, *theirs = refs
    incoming = incoming_of(bits, place_ref, col_ref, held_ref, got)
    for start in range(0, col_ref.shape[0], NORM_BLOCK):
        here = slice(start, start + NORM_BLOCK)
        joins = col_ref[here, :] == col_ref[:1, :]
        for k in range(groups):
            width = queries[k].shape[1]
            for g in range(width // HEAD):
                cut = slice(g * HEAD, (g + 1) * HEAD)
                out = slice(k * width + g * HEAD, k * width + (g + 1) * HEAD)
                carried = dot(queries[k][here, cut], incoming[k * HEAD : (k + 1) * HEAD, :])
                combined = intras[k][here, cut] + jnp.where(joins, carried, 0.0)
                scale = lax.rsqrt(jnp.mean(combined * combined, axis=-1, keepdims=True) + EPSILON)
                normed_ref[here, out] = (combined * scale * gain_ref[:1, out]).astype(BF16)
    product = dot(normed_ref[...], columns(weight_ref, 1 - core_ref[0])).astype(BF16)
    size = theirs[0].shape[0]
    for i, part in enumerate(theirs):
        part[...] = product[i * size : (i + 1) * size, :]


def columns(weight_ref, part):
    half = weight_ref.shape[1] // 2
    return weight_ref[:, pl.ds(pl.multiple_of(part * half, half), half)]


def own_kernel(core_ref, normed_ref, weight_ref, out_ref):
    out_ref[...] = dot(normed_ref[...], columns(weight_ref, core_ref[0]))


def add_kernel(mine_ref, theirs_ref, *refs):
    out_ref = refs[-1]
    size = out_ref.shape[0]
    step = pl.program_id(0)
    first = pl.multiple_of((step + (pl.num_programs(0) if len(refs) > 1 else 0)) * size, size)
    here = pl.ds(pl.multiple_of(step * size, size), size)
    out_ref[...] = (mine_ref[pl.ds(first, size), :] + theirs_ref[here, :].astype(F32)).astype(BF16)


def shape(dims, dtype):
    return jax.ShapeDtypeStruct(dims, dtype)


def in_hbm(x):
    return pltpu.with_memory_space_constraint(x, pltpu.HBM)


def swap_head(x):
    return lax.ppermute(x, "head", [(0, 1), (1, 0)])


def on_device(tokens, q_weight, key_matrix, value_matrix, norm_gain, out_weight, doc_ids):
    rows, half = tokens.shape
    kv_width = key_matrix.shape[1]
    q_width = q_weight.shape[1]
    kv_heads = kv_width // HEAD
    group_width = q_width // kv_heads
    state_rows = kv_heads * HEAD
    count = lax.axis_size("seq")
    core = lax.axis_index("head").astype(jnp.int32).reshape(1)
    place = lax.axis_index("seq").astype(jnp.int32).reshape(1)
    other = swap_head(tokens)
    gain = norm_gain.reshape(1, q_width)
    own, wk, wv, k_part, v_part, col, row = pl.pallas_call(
        own_half_kernel,
        out_shape=(
            shape(tokens.shape, BF16),
            shape(key_matrix.shape, BF16),
            shape(value_matrix.shape, BF16),
            shape((rows, kv_width), F32),
            shape((rows, kv_width), F32),
            shape((rows, HEAD), F32),
            shape((8, rows), F32),
        ),
        in_specs=[SMEM, HBM, HBM, HBM, HBM],
        out_specs=(VMEM,) * 7,
        scratch_shapes=[pltpu.VMEM((1, rows), jnp.int32), pltpu.SemaphoreType.DMA((3 * CHUNKS + 3,))],
        compiler_params=params(8),
        name="own_half",
    )(core, *(in_hbm(x) for x in (doc_ids.reshape(1, rows), tokens, key_matrix, value_matrix)))

    key, value, message = pl.pallas_call(
        key_value_kernel,
        out_shape=(
            shape((rows, kv_width), BF16),
            shape((rows, kv_width), BF16),
            shape((state_rows + ID_ROWS, HEAD), BF16),
        ),
        in_specs=[SMEM] + [VMEM] * 6,
        out_specs=(VMEM, VMEM, VMEM),
        compiler_params=params(16),
        name="key_value",
    )(core, other, k_part, v_part, wk, wv, col)

    def intra(k, key, value):
        return pl.pallas_call(
            intra_kernel,
            out_shape=(shape((rows, group_width), BF16), shape((rows, group_width), F32)),
            grid=(1,),
            in_specs=[
                SMEM,
                VMEM,
                VMEM,
                pl.BlockSpec((2 * half, group_width), lambda i: (0, k)),
                pl.BlockSpec((rows, HEAD), lambda i: (0, k)),
                pl.BlockSpec((rows, HEAD), lambda i: (0, k)),
                VMEM,
                VMEM,
            ],
            out_specs=(VMEM, VMEM),
            compiler_params=params(24),
            name=f"intra_{k}",
        )(core, own, other, wq, key, value, col, row)

    held = None
    queries, intras = [], []
    for step, bits in enumerate(ROUNDS):
        final = step == len(ROUNDS) - 1
        got = [lax.ppermute(message, "seq", [(i, i ^ b) for i in range(count)]) for b in bits]
        if step == 0:
            wq = pl.pallas_call(
                stage_kernel,
                out_shape=shape(q_weight.shape, BF16),
                in_specs=[VMEM, HBM],
                out_specs=VMEM,
                scratch_shapes=[pltpu.SemaphoreType.DMA((STAGE_COPIES,))],
                compiler_params=params(2),
                name="stage",
            )(message, in_hbm(q_weight))
        if step in INTRA_STEPS:
            (key, value), _ = lax.optimization_barrier(((key, value), message))
            query, part = intra(INTRA_STEPS.index(step), key, value)
            queries.append(query)
            intras.append(part)
        if final:
            break
        extra = () if held is None else (held,)
        message, held = pl.pallas_call(
            lambda *refs, bits=bits, has=held is not None: combine_kernel(bits, has, *refs),
            out_shape=(shape(message.shape, BF16), shape((state_rows, HEAD), F32)),
            in_specs=[SMEM] + [VMEM] * (2 + len(bits) + len(extra)),
            out_specs=(VMEM, VMEM),
            compiler_params=params(4),
            name="combine",
        )(place, col, message, *got, *extra)
        if step == 0:
            message, wq = lax.optimization_barrier((message, wq))
        if step in INTRA_STEPS:
            message, queries[-1] = lax.optimization_barrier((message, queries[-1]))

    normed, *theirs = pl.pallas_call(
        lambda *refs: norm_kernel(ROUNDS[-1], kv_heads, *refs),
        out_shape=(shape((rows, q_width), BF16),) + (shape((BLOCK, half), BF16),) * (rows // BLOCK),
        in_specs=[SMEM, SMEM] + [VMEM] * (1 + len(got) + 2 * kv_heads + 3),
        out_specs=(VMEM,) * (1 + rows // BLOCK),
        compiler_params=params(16),
        name="norm",
    )(core, place, held, *got, *queries, *intras, col, gain, out_weight)
    received = [swap_head(part) for part in theirs]
    mine = pl.pallas_call(
        own_kernel,
        out_shape=shape((rows, half), F32),
        in_specs=[SMEM, VMEM, VMEM],
        out_specs=VMEM,
        compiler_params=params(16),
        name="own",
    )(core, normed, out_weight)
    out = ()
    for part in range(rows // BLOCK):
        out = (
            pl.pallas_call(
                add_kernel,
                grid=(ADD_STEPS,),
                out_shape=shape((rows, half), BF16),
                in_specs=[VMEM, VMEM] + [HBM] * len(out),
                out_specs=pl.BlockSpec(
                    (BLOCK // ADD_STEPS, half), lambda i, part=part: (i + part * ADD_STEPS, 0)
                ),
                input_output_aliases={2: 0} if out else {},
                compiler_params=params(8),
                name=f"add_{part}",
            )(mine, received[part], *out),
        )
    return out[0]


def solution(mesh):
    return jax.shard_map(
        on_device,
        mesh=mesh,
        in_specs=(
            P("seq", "head"),
            P(None, "head"),
            P(None, "head"),
            P(None, "head"),
            P("head"),
            P("head", None),
            P("seq"),
        ),
        out_specs=P("seq", "head"),
        check_vma=False,
    )
```

```python
import jax
import jax.numpy as jnp
from jax import lax
from jax.experimental import pallas as pl
from jax.experimental.pallas import tpu as pltpu
from jax.sharding import PartitionSpec as P

HEAD = 128
ID_ROWS = 16
BLOCK = 256
NORM_BLOCK = 512
ROUNDS = ((1, 2, 3), (6,), (8, 24, 16), (32, 64, 96))
INTRA_STEPS = (1, 2)
CHUNKS = 2
STAGE_COPIES = 4
ADD_STEPS = 2
EPSILON = 1e-05
F32 = jnp.float32
BF16 = jnp.bfloat16

SMEM = pl.BlockSpec(memory_space=pltpu.SMEM)
VMEM = pl.BlockSpec(memory_space=pltpu.VMEM)
HBM = pl.BlockSpec(memory_space=pltpu.HBM)


def params(mib):
    return pltpu.CompilerParams(vmem_limit_bytes=mib << 20)


def dot(a, b):
    return jnp.dot(a, b, preferred_element_type=F32)


def features(x):
    return jnp.where(x > 0.0, x + 1.0, jnp.exp(jnp.minimum(x, 0.0)))


def project(core_ref, own_ref, other_ref, weight_ref):
    half = own_ref.shape[1]
    mine = pl.multiple_of(core_ref[0] * half, half)
    theirs = pl.multiple_of((1 - core_ref[0]) * half, half)
    return dot(own_ref[...], weight_ref[pl.ds(mine, half), :]) + dot(
        other_ref[...], weight_ref[pl.ds(theirs, half), :]
    )


def own_half_kernel(core_ref, ids_hbm, own_hbm, wk_hbm, wv_hbm, *refs):
    own_ref, wk_ref, wv_ref, k_ref, v_ref, col_ref, row_ref, ids_vmem, sems = refs
    half = own_hbm.shape[1]
    chunk = half // CHUNKS
    near = core_ref[0] * half
    far = pl.multiple_of((1 - core_ref[0]) * half, half)
    copies = []
    for c in range(CHUNKS):
        cut = pl.ds(pl.multiple_of(near + c * chunk, chunk), chunk)
        copies.append((own_hbm.at[:, c * chunk : (c + 1) * chunk], own_ref.at[:, c * chunk : (c + 1) * chunk]))
        copies.append((wk_hbm.at[cut, :], wk_ref.at[cut, :]))
        copies.append((wv_hbm.at[cut, :], wv_ref.at[cut, :]))
    cut = pl.ds(far, half)
    copies.append((wk_hbm.at[cut, :], wk_ref.at[cut, :]))
    copies.append((wv_hbm.at[cut, :], wv_ref.at[cut, :]))
    copies.insert(0, (ids_hbm, ids_vmem))
    copies = [pltpu.make_async_copy(a, b, sems.at[i]) for i, (a, b) in enumerate(copies)]
    for copy in copies:
        copy.start()
    copies[0].wait()
    ids = ids_vmem[...].astype(F32)
    row_ref[...] = jnp.broadcast_to(ids, row_ref.shape)
    col_ref[...] = jnp.broadcast_to(ids, (HEAD, ids.shape[1])).T
    for c in range(CHUNKS):
        for copy in copies[3 * c + 1 : 3 * c + 4]:
            copy.wait()
        own = own_ref[:, c * chunk : (c + 1) * chunk]
        cut = pl.ds(pl.multiple_of(near + c * chunk, chunk), chunk)
        key = dot(own, wk_ref[cut, :])
        value = dot(own, wv_ref[cut, :])
        if c == 0:
            k_ref[...] = key
            v_ref[...] = value
        else:
            k_ref[...] += key
            v_ref[...] += value
    for copy in copies[3 * CHUNKS + 1 :]:
        copy.wait()


def key_value_kernel(core_ref, other_ref, k_part_ref, v_part_ref, wk_ref, wv_ref, col_ref, *outs):
    k_ref, v_ref, message_ref = outs
    rows, half = other_ref.shape
    other = other_ref[...]
    far = pl.ds(pl.multiple_of((1 - core_ref[0]) * half, half), half)
    key = features(k_part_ref[...] + dot(other, wk_ref[far, :])).astype(BF16)
    value = (v_part_ref[...] + dot(other, wv_ref[far, :])).astype(BF16)
    k_ref[...] = key
    v_ref[...] = value
    last = col_ref[rows - 1 : rows, :]
    tail = col_ref[...] == last
    heads = key.shape[1] // HEAD
    for h in range(heads):
        cut = slice(h * HEAD, (h + 1) * HEAD)
        tail_key = jnp.where(tail, key[:, cut].astype(F32), 0.0).astype(BF16)
        state = lax.dot_general(
            tail_key, value[:, cut], (((0,), (0,)), ((), ())), preferred_element_type=F32
        )
        message_ref[cut, :] = state.astype(BF16)
    message_ref[heads * HEAD :, :] = jnp.broadcast_to(last, (ID_ROWS, HEAD)).astype(BF16)


def stage_kernel(after_ref, weight_hbm, weight_ref, sems):
    size = weight_ref.shape[0] // STAGE_COPIES
    copies = []
    for i in range(STAGE_COPIES):
        cut = slice(i * size, (i + 1) * size)
        copies.append(pltpu.make_async_copy(weight_hbm.at[cut, :], weight_ref.at[cut, :], sems.at[i]))
    for copy in copies:
        copy.start()
    for copy in copies:
        copy.wait()


def intra_kernel(core_ref, own_ref, other_ref, wq_ref, k_ref, v_ref, col_ref, row_ref, q_ref, intra_ref):
    rows = own_ref.shape[0]
    group = wq_ref.shape[1] // HEAD
    q_ref[...] = features(project(core_ref, own_ref, other_ref, wq_ref)).astype(BF16)
    for start in range(0, rows, BLOCK):
        seen = start + BLOCK
        here = slice(start, seen)
        key = k_ref[:seen, :]
        value = v_ref[:seen, :]
        t = lax.broadcasted_iota(jnp.int32, (BLOCK, seen), 0) + start
        s = lax.broadcasted_iota(jnp.int32, (BLOCK, seen), 1)
        same = (col_ref[here, :1] == row_ref[:1, :seen]) & (t >= s)
        for g in range(group):
            cut = slice(g * HEAD, (g + 1) * HEAD)
            scores = lax.dot_general(
                q_ref[here, cut], key, (((1,), (1,)), ((), ())), preferred_element_type=F32
            )
            scores = jnp.where(same, scores, 0.0).astype(BF16)
            intra_ref[here, cut] = dot(scores, value)


def combine_kernel(bits, has_held, place_ref, col_ref, message_ref, *refs):
    got = refs[: len(bits)]
    held_in = refs[len(bits)] if has_held else None
    next_ref, held_ref = refs[-2:]
    rows = message_ref.shape[0] - ID_ROWS
    own_id = message_ref[rows : rows + 1, :].astype(F32)
    ids = [g[rows : rows + 1, :].astype(F32) for g in got]
    top = own_id
    for i in ids:
        top = jnp.maximum(top, i)
    first = col_ref[:1, :]
    total = jnp.where(own_id == top, message_ref[:rows, :].astype(F32), 0.0)
    held = held_in[...] if has_held else jnp.zeros((rows, HEAD), F32)
    for b, g, i in zip(bits, got, ids):
        state = g[:rows, :].astype(F32)
        earlier = (place_ref[0] & (1 << (b.bit_length() - 1))) != 0
        held = held + jnp.where((i == first) & earlier, state, 0.0)
        total = total + jnp.where(i == top, state, 0.0)
    next_ref[:rows, :] = total.astype(BF16)
    next_ref[rows:, :] = jnp.broadcast_to(top, (ID_ROWS, HEAD)).astype(BF16)
    held_ref[...] = held


def incoming_of(bits, place_ref, col_ref, held_ref, got):
    first = col_ref[:1, :]
    rows = held_ref.shape[0]
    held = held_ref[...]
    for b, g in zip(bits, got):
        earlier = (place_ref[0] & (1 << (b.bit_length() - 1))) != 0
        same = (g[rows : rows + 1, :].astype(F32) == first) & earlier
        held = held + jnp.where(same, g[:rows, :].astype(F32), 0.0)
    return held.astype(BF16)


def norm_kernel(bits, groups, core_ref, place_ref, held_ref, *refs):
    got, refs = refs[: len(bits)], refs[len(bits) :]
    queries, intras, refs = refs[:groups], refs[groups : 2 * groups], refs[2 * groups :]
    col_ref, gain_ref, weight_ref, normed_ref, *theirs = refs
    incoming = incoming_of(bits, place_ref, col_ref, held_ref, got)
    for start in range(0, col_ref.shape[0], NORM_BLOCK):
        here = slice(start, start + NORM_BLOCK)
        joins = col_ref[here, :] == col_ref[:1, :]
        for k in range(groups):
            width = queries[k].shape[1]
            for g in range(width // HEAD):
                cut = slice(g * HEAD, (g + 1) * HEAD)
                out = slice(k * width + g * HEAD, k * width + (g + 1) * HEAD)
                carried = dot(queries[k][here, cut], incoming[k * HEAD : (k + 1) * HEAD, :])
                combined = intras[k][here, cut] + jnp.where(joins, carried, 0.0)
                scale = lax.rsqrt(jnp.mean(combined * combined, axis=-1, keepdims=True) + EPSILON)
                normed_ref[here, out] = (combined * scale * gain_ref[:1, out]).astype(BF16)
    product = dot(normed_ref[...], columns(weight_ref, 1 - core_ref[0])).astype(BF16)
    size = theirs[0].shape[0]
    for i, part in enumerate(theirs):
        part[...] = product[i * size : (i + 1) * size, :]


def columns(weight_ref, part):
    half = weight_ref.shape[1] // 2
    return weight_ref[:, pl.ds(pl.multiple_of(part * half, half), half)]


def own_kernel(core_ref, normed_ref, weight_ref, out_ref):
    out_ref[...] = dot(normed_ref[...], columns(weight_ref, core_ref[0]))


def add_kernel(mine_ref, theirs_ref, *refs):
    out_ref = refs[-1]
    size = out_ref.shape[0]
    step = pl.program_id(0)
    first = pl.multiple_of((step + (pl.num_programs(0) if len(refs) > 1 else 0)) * size, size)
    here = pl.ds(pl.multiple_of(step * size, size), size)
    out_ref[...] = (mine_ref[pl.ds(first, size), :] + theirs_ref[here, :].astype(F32)).astype(BF16)


def shape(dims, dtype):
    return jax.ShapeDtypeStruct(dims, dtype)


def in_hbm(x):
    return pltpu.with_memory_space_constraint(x, pltpu.HBM)


def swap_head(x):
    return lax.ppermute(x, "head", [(0, 1), (1, 0)])


def on_device(tokens, q_weight, key_matrix, value_matrix, norm_gain, out_weight, doc_ids):
    rows, half = tokens.shape
    kv_width = key_matrix.shape[1]
    q_width = q_weight.shape[1]
    kv_heads = kv_width // HEAD
    group_width = q_width // kv_heads
    state_rows = kv_heads * HEAD
    count = lax.axis_size("seq")
    core = lax.axis_index("head").astype(jnp.int32).reshape(1)
    place = lax.axis_index("seq").astype(jnp.int32).reshape(1)
    other = swap_head(tokens)
    gain = norm_gain.reshape(1, q_width)
    own, wk, wv, k_part, v_part, col, row = pl.pallas_call(
        own_half_kernel,
        out_shape=(
            shape(tokens.shape, BF16),
            shape(key_matrix.shape, BF16),
            shape(value_matrix.shape, BF16),
            shape((rows, kv_width), F32),
            shape((rows, kv_width), F32),
            shape((rows, HEAD), F32),
            shape((8, rows), F32),
        ),
        in_specs=[SMEM, HBM, HBM, HBM, HBM],
        out_specs=(VMEM,) * 7,
        scratch_shapes=[pltpu.VMEM((1, rows), jnp.int32), pltpu.SemaphoreType.DMA((3 * CHUNKS + 3,))],
        compiler_params=params(8),
        name="own_half",
    )(core, *(in_hbm(x) for x in (doc_ids.reshape(1, rows), tokens, key_matrix, value_matrix)))

    key, value, message = pl.pallas_call(
        key_value_kernel,
        out_shape=(
            shape((rows, kv_width), BF16),
            shape((rows, kv_width), BF16),
            shape((state_rows + ID_ROWS, HEAD), BF16),
        ),
        in_specs=[SMEM] + [VMEM] * 6,
        out_specs=(VMEM, VMEM, VMEM),
        compiler_params=params(16),
        name="key_value",
    )(core, other, k_part, v_part, wk, wv, col)

    def intra(k, key, value):
        return pl.pallas_call(
            intra_kernel,
            out_shape=(shape((rows, group_width), BF16), shape((rows, group_width), F32)),
            grid=(1,),
            in_specs=[
                SMEM,
                VMEM,
                VMEM,
                pl.BlockSpec((2 * half, group_width), lambda i: (0, k)),
                pl.BlockSpec((rows, HEAD), lambda i: (0, k)),
                pl.BlockSpec((rows, HEAD), lambda i: (0, k)),
                VMEM,
                VMEM,
            ],
            out_specs=(VMEM, VMEM),
            compiler_params=params(24),
            name=f"intra_{k}",
        )(core, own, other, wq, key, value, col, row)

    held = None
    queries, intras = [], []
    for step, bits in enumerate(ROUNDS):
        final = step == len(ROUNDS) - 1
        got = [
            lax.ppermute(
                message,
                "seq",
                [(i, i ^ b) for i in range(count) if not (final and 4 * i >= 3 * count > 12 * (i ^ b))],
            )
            for b in bits
        ]
        if step == 0:
            wq = pl.pallas_call(
                stage_kernel,
                out_shape=shape(q_weight.shape, BF16),
                in_specs=[VMEM, HBM],
                out_specs=VMEM,
                scratch_shapes=[pltpu.SemaphoreType.DMA((STAGE_COPIES,))],
                compiler_params=params(2),
                name="stage",
            )(message, in_hbm(q_weight))
        if step in INTRA_STEPS:
            (key, value), _ = lax.optimization_barrier(((key, value), message))
            query, part = intra(INTRA_STEPS.index(step), key, value)
            queries.append(query)
            intras.append(part)
        if final:
            break
        extra = () if held is None else (held,)
        message, held = pl.pallas_call(
            lambda *refs, bits=bits, has=held is not None: combine_kernel(bits, has, *refs),
            out_shape=(shape(message.shape, BF16), shape((state_rows, HEAD), F32)),
            in_specs=[SMEM] + [VMEM] * (2 + len(bits) + len(extra)),
            out_specs=(VMEM, VMEM),
            compiler_params=params(4),
            name="combine",
        )(place, col, message, *got, *extra)
        if step == 0:
            message, wq = lax.optimization_barrier((message, wq))
        if step in INTRA_STEPS:
            message, queries[-1] = lax.optimization_barrier((message, queries[-1]))

    normed, *theirs = pl.pallas_call(
        lambda *refs: norm_kernel(ROUNDS[-1], kv_heads, *refs),
        out_shape=(shape((rows, q_width), BF16),) + (shape((BLOCK, half), BF16),) * (rows // BLOCK),
        in_specs=[SMEM, SMEM] + [VMEM] * (1 + len(got) + 2 * kv_heads + 3),
        out_specs=(VMEM,) * (1 + rows // BLOCK),
        compiler_params=params(16),
        name="norm",
    )(core, place, held, *got, *queries, *intras, col, gain, out_weight)
    received = [swap_head(part) for part in theirs]
    mine = pl.pallas_call(
        own_kernel,
        out_shape=shape((rows, half), F32),
        in_specs=[SMEM, VMEM, VMEM],
        out_specs=VMEM,
        compiler_params=params(16),
        name="own",
    )(core, normed, out_weight)
    out = ()
    for part in range(rows // BLOCK):
        out = (
            pl.pallas_call(
                add_kernel,
                grid=(ADD_STEPS,),
                out_shape=shape((rows, half), BF16),
                in_specs=[VMEM, VMEM] + [HBM] * len(out),
                out_specs=pl.BlockSpec(
                    (BLOCK // ADD_STEPS, half), lambda i, part=part: (i + part * ADD_STEPS, 0)
                ),
                input_output_aliases={2: 0} if out else {},
                compiler_params=params(8),
                name=f"add_{part}",
            )(mine, received[part], *out),
        )
    return out[0]


def solution(mesh):
    return jax.shard_map(
        on_device,
        mesh=mesh,
        in_specs=(
            P("seq", "head"),
            P(None, "head"),
            P(None, "head"),
            P(None, "head"),
            P("head"),
            P("head", None),
            P("seq"),
        ),
        out_specs=P("seq", "head"),
        check_vma=False,
    )
```

```python
import jax
import jax.numpy as jnp
from jax import lax
from jax.experimental import pallas as pl
from jax.experimental.pallas import tpu as pltpu
from jax.sharding import PartitionSpec as P

HEAD = 128
ID_ROWS = 8
BLOCK = 256
NORM_BLOCK = 512
ROUNDS = ((1, 2, 3), (6,), (8, 24, 16), (32, 96, 64))
INTRA_STEPS = (1, 3)
CHUNKS = 2
STAGE_COPIES = 4
ADD_STEPS = 2
EPSILON = 1e-05
F32 = jnp.float32
BF16 = jnp.bfloat16

SMEM = pl.BlockSpec(memory_space=pltpu.SMEM)
VMEM = pl.BlockSpec(memory_space=pltpu.VMEM)
HBM = pl.BlockSpec(memory_space=pltpu.HBM)


def params(mib):
    return pltpu.CompilerParams(vmem_limit_bytes=mib << 20)


def dot(a, b):
    return jnp.dot(a, b, preferred_element_type=F32)


def features(x):
    return jnp.where(x > 0.0, x + 1.0, jnp.exp(jnp.minimum(x, 0.0)))


def project(core_ref, own_ref, other_ref, weight_ref):
    half = own_ref.shape[1]
    mine = pl.multiple_of(core_ref[0] * half, half)
    theirs = pl.multiple_of((1 - core_ref[0]) * half, half)
    return dot(own_ref[...], weight_ref[pl.ds(mine, half), :]) + dot(
        other_ref[...], weight_ref[pl.ds(theirs, half), :]
    )


def own_half_kernel(core_ref, ids_hbm, own_hbm, wk_hbm, wv_hbm, *refs):
    own_ref, wk_ref, wv_ref, k_ref, v_ref, col_ref, row_ref, ids_vmem, sems = refs
    half = own_hbm.shape[1]
    chunk = half // CHUNKS
    near = core_ref[0] * half
    far = pl.multiple_of((1 - core_ref[0]) * half, half)
    copies = []
    for c in range(CHUNKS):
        cut = pl.ds(pl.multiple_of(near + c * chunk, chunk), chunk)
        copies.append((own_hbm.at[:, c * chunk : (c + 1) * chunk], own_ref.at[:, c * chunk : (c + 1) * chunk]))
        copies.append((wk_hbm.at[cut, :], wk_ref.at[cut, :]))
        copies.append((wv_hbm.at[cut, :], wv_ref.at[cut, :]))
    cut = pl.ds(far, half)
    copies.append((wk_hbm.at[cut, :], wk_ref.at[cut, :]))
    copies.append((wv_hbm.at[cut, :], wv_ref.at[cut, :]))
    copies.insert(0, (ids_hbm, ids_vmem))
    copies = [pltpu.make_async_copy(a, b, sems.at[i]) for i, (a, b) in enumerate(copies)]
    for copy in copies:
        copy.start()
    copies[0].wait()
    ids = ids_vmem[...].astype(F32)
    row_ref[...] = jnp.broadcast_to(ids, row_ref.shape)
    col_ref[...] = jnp.broadcast_to(ids, (HEAD, ids.shape[1])).T
    for c in range(CHUNKS):
        for copy in copies[3 * c + 1 : 3 * c + 4]:
            copy.wait()
        own = own_ref[:, c * chunk : (c + 1) * chunk]
        cut = pl.ds(pl.multiple_of(near + c * chunk, chunk), chunk)
        key = dot(own, wk_ref[cut, :])
        value = dot(own, wv_ref[cut, :])
        if c == 0:
            k_ref[...] = key
            v_ref[...] = value
        else:
            k_ref[...] += key
            v_ref[...] += value
    for copy in copies[3 * CHUNKS + 1 :]:
        copy.wait()


def key_value_kernel(core_ref, other_ref, k_part_ref, v_part_ref, wk_ref, wv_ref, col_ref, *outs):
    k_ref, v_ref, message_ref = outs
    rows, half = other_ref.shape
    other = other_ref[...]
    far = pl.ds(pl.multiple_of((1 - core_ref[0]) * half, half), half)
    key = features(k_part_ref[...] + dot(other, wk_ref[far, :])).astype(BF16)
    value = (v_part_ref[...] + dot(other, wv_ref[far, :])).astype(BF16)
    k_ref[...] = key
    v_ref[...] = value
    last = col_ref[rows - 1 : rows, :]
    tail = col_ref[...] == last
    heads = key.shape[1] // HEAD
    for h in range(heads):
        cut = slice(h * HEAD, (h + 1) * HEAD)
        tail_key = jnp.where(tail, key[:, cut].astype(F32), 0.0).astype(BF16)
        state = lax.dot_general(
            tail_key, value[:, cut], (((0,), (0,)), ((), ())), preferred_element_type=F32
        )
        message_ref[cut, :] = state.astype(BF16)
    message_ref[heads * HEAD :, :] = jnp.broadcast_to(last, (ID_ROWS, HEAD)).astype(BF16)


def stage_kernel(after_ref, weight_hbm, weight_ref, sems):
    size = weight_ref.shape[0] // STAGE_COPIES
    copies = []
    for i in range(STAGE_COPIES):
        cut = slice(i * size, (i + 1) * size)
        copies.append(pltpu.make_async_copy(weight_hbm.at[cut, :], weight_ref.at[cut, :], sems.at[i]))
    for copy in copies:
        copy.start()
    for copy in copies:
        copy.wait()


def intra_kernel(core_ref, own_ref, other_ref, wq_ref, k_ref, v_ref, col_ref, row_ref, q_ref, intra_ref):
    rows = own_ref.shape[0]
    group = wq_ref.shape[1] // HEAD
    q_ref[...] = features(project(core_ref, own_ref, other_ref, wq_ref)).astype(BF16)
    for start in range(0, rows, BLOCK):
        seen = start + BLOCK
        here = slice(start, seen)
        key = k_ref[:seen, :]
        value = v_ref[:seen, :]
        t = lax.broadcasted_iota(jnp.int32, (BLOCK, seen), 0) + start
        s = lax.broadcasted_iota(jnp.int32, (BLOCK, seen), 1)
        same = (col_ref[here, :1] == row_ref[:1, :seen]) & (t >= s)
        for g in range(group):
            cut = slice(g * HEAD, (g + 1) * HEAD)
            scores = lax.dot_general(
                q_ref[here, cut], key, (((1,), (1,)), ((), ())), preferred_element_type=F32
            )
            scores = jnp.where(same, scores, 0.0).astype(BF16)
            intra_ref[here, cut] = dot(scores, value)


def combine_kernel(bits, has_held, place_ref, col_ref, message_ref, *refs):
    got = refs[: len(bits)]
    held_in = refs[len(bits)] if has_held else None
    next_ref, held_ref = refs[-2:]
    rows = message_ref.shape[0] - ID_ROWS
    own_id = message_ref[rows : rows + 1, :].astype(F32)
    ids = [g[rows : rows + 1, :].astype(F32) for g in got]
    top = own_id
    for i in ids:
        top = jnp.maximum(top, i)
    first = col_ref[:1, :]
    total = jnp.where(own_id == top, message_ref[:rows, :].astype(F32), 0.0)
    held = held_in[...] if has_held else jnp.zeros((rows, HEAD), F32)
    for b, g, i in zip(bits, got, ids):
        state = g[:rows, :].astype(F32)
        earlier = (place_ref[0] & (1 << (b.bit_length() - 1))) != 0
        held = held + jnp.where((i == first) & earlier, state, 0.0)
        total = total + jnp.where(i == top, state, 0.0)
    next_ref[:rows, :] = total.astype(BF16)
    next_ref[rows:, :] = jnp.broadcast_to(top, (ID_ROWS, HEAD)).astype(BF16)
    held_ref[...] = held


def incoming_of(bits, place_ref, col_ref, held_ref, got):
    first = col_ref[:1, :]
    rows = held_ref.shape[0]
    held = held_ref[...]
    for b, g in zip(bits, got):
        earlier = (place_ref[0] & (1 << (b.bit_length() - 1))) != 0
        same = (g[rows : rows + 1, :].astype(F32) == first) & earlier
        held = held + jnp.where(same, g[:rows, :].astype(F32), 0.0)
    return held.astype(BF16)


def norm_kernel(bits, groups, core_ref, place_ref, held_ref, *refs):
    got, refs = refs[: len(bits)], refs[len(bits) :]
    queries, intras, refs = refs[:groups], refs[groups : 2 * groups], refs[2 * groups :]
    col_ref, gain_ref, weight_ref, normed_ref, *theirs = refs
    incoming = incoming_of(bits, place_ref, col_ref, held_ref, got)
    for start in range(0, col_ref.shape[0], NORM_BLOCK):
        here = slice(start, start + NORM_BLOCK)
        joins = col_ref[here, :] == col_ref[:1, :]
        for k in range(groups):
            width = queries[k].shape[1]
            for g in range(width // HEAD):
                cut = slice(g * HEAD, (g + 1) * HEAD)
                out = slice(k * width + g * HEAD, k * width + (g + 1) * HEAD)
                carried = dot(queries[k][here, cut], incoming[k * HEAD : (k + 1) * HEAD, :])
                combined = intras[k][here, cut] + jnp.where(joins, carried, 0.0)
                scale = lax.rsqrt(jnp.mean(combined * combined, axis=-1, keepdims=True) + EPSILON)
                normed_ref[here, out] = (combined * scale * gain_ref[:1, out]).astype(BF16)
    product = dot(normed_ref[...], columns(weight_ref, 1 - core_ref[0])).astype(BF16)
    size = theirs[0].shape[0]
    for i, part in enumerate(theirs):
        part[...] = product[i * size : (i + 1) * size, :]


def columns(weight_ref, part):
    half = weight_ref.shape[1] // 2
    return weight_ref[:, pl.ds(pl.multiple_of(part * half, half), half)]


def own_kernel(core_ref, normed_ref, weight_ref, out_ref):
    out_ref[...] = dot(normed_ref[...], columns(weight_ref, core_ref[0]))


def add_kernel(mine_ref, theirs_ref, *refs):
    out_ref = refs[-1]
    size = out_ref.shape[0]
    step = pl.program_id(0)
    first = pl.multiple_of((step + (pl.num_programs(0) if len(refs) > 1 else 0)) * size, size)
    here = pl.ds(pl.multiple_of(step * size, size), size)
    out_ref[...] = (mine_ref[pl.ds(first, size), :] + theirs_ref[here, :].astype(F32)).astype(BF16)


def shape(dims, dtype):
    return jax.ShapeDtypeStruct(dims, dtype)


def in_hbm(x):
    return pltpu.with_memory_space_constraint(x, pltpu.HBM)


def swap_head(x):
    return lax.ppermute(x, "head", [(0, 1), (1, 0)])


def on_device(tokens, q_weight, key_matrix, value_matrix, norm_gain, out_weight, doc_ids):
    rows, half = tokens.shape
    kv_width = key_matrix.shape[1]
    q_width = q_weight.shape[1]
    kv_heads = kv_width // HEAD
    group_width = q_width // kv_heads
    state_rows = kv_heads * HEAD
    count = lax.axis_size("seq")
    core = lax.axis_index("head").astype(jnp.int32).reshape(1)
    place = lax.axis_index("seq").astype(jnp.int32).reshape(1)
    other = swap_head(tokens)
    gain = norm_gain.reshape(1, q_width)
    own, wk, wv, k_part, v_part, col, row = pl.pallas_call(
        own_half_kernel,
        out_shape=(
            shape(tokens.shape, BF16),
            shape(key_matrix.shape, BF16),
            shape(value_matrix.shape, BF16),
            shape((rows, kv_width), F32),
            shape((rows, kv_width), F32),
            shape((rows, HEAD), F32),
            shape((8, rows), F32),
        ),
        in_specs=[SMEM, HBM, HBM, HBM, HBM],
        out_specs=(VMEM,) * 7,
        scratch_shapes=[pltpu.VMEM((1, rows), jnp.int32), pltpu.SemaphoreType.DMA((3 * CHUNKS + 3,))],
        compiler_params=params(8),
        name="own_half",
    )(core, *(in_hbm(x) for x in (doc_ids.reshape(1, rows), tokens, key_matrix, value_matrix)))

    key, value, message = pl.pallas_call(
        key_value_kernel,
        out_shape=(
            shape((rows, kv_width), BF16),
            shape((rows, kv_width), BF16),
            shape((state_rows + ID_ROWS, HEAD), BF16),
        ),
        in_specs=[SMEM] + [VMEM] * 6,
        out_specs=(VMEM, VMEM, VMEM),
        compiler_params=params(16),
        name="key_value",
    )(core, other, k_part, v_part, wk, wv, col)

    def intra(k, key, value):
        return pl.pallas_call(
            intra_kernel,
            out_shape=(shape((rows, group_width), BF16), shape((rows, group_width), F32)),
            grid=(1,),
            in_specs=[
                SMEM,
                VMEM,
                VMEM,
                pl.BlockSpec((2 * half, group_width), lambda i: (0, k)),
                pl.BlockSpec((rows, HEAD), lambda i: (0, k)),
                pl.BlockSpec((rows, HEAD), lambda i: (0, k)),
                VMEM,
                VMEM,
            ],
            out_specs=(VMEM, VMEM),
            compiler_params=params(24),
            name=f"intra_{k}",
        )(core, own, other, wq, key, value, col, row)

    held = None
    queries, intras = [], []
    for step, bits in enumerate(ROUNDS):
        final = step == len(ROUNDS) - 1
        got = [lax.ppermute(message, "seq", [(i, i ^ b) for i in range(count)]) for b in bits]
        if step == 0:
            wq = pl.pallas_call(
                stage_kernel,
                out_shape=shape(q_weight.shape, BF16),
                in_specs=[VMEM, HBM],
                out_specs=VMEM,
                scratch_shapes=[pltpu.SemaphoreType.DMA((STAGE_COPIES,))],
                compiler_params=params(2),
                name="stage",
            )(message, in_hbm(q_weight))
        if step in INTRA_STEPS:
            (key, value), _ = lax.optimization_barrier(((key, value), message))
            query, part = intra(INTRA_STEPS.index(step), key, value)
            queries.append(query)
            intras.append(part)
        if final:
            break
        extra = () if held is None else (held,)
        message, held = pl.pallas_call(
            lambda *refs, bits=bits, has=held is not None: combine_kernel(bits, has, *refs),
            out_shape=(shape(message.shape, BF16), shape((state_rows, HEAD), F32)),
            in_specs=[SMEM] + [VMEM] * (2 + len(bits) + len(extra)),
            out_specs=(VMEM, VMEM),
            compiler_params=params(4),
            name="combine",
        )(place, col, message, *got, *extra)
        if step == 0:
            message, wq = lax.optimization_barrier((message, wq))
        if step in INTRA_STEPS and not final:
            message, queries[-1] = lax.optimization_barrier((message, queries[-1]))

    normed, *theirs = pl.pallas_call(
        lambda *refs: norm_kernel(ROUNDS[-1], kv_heads, *refs),
        out_shape=(shape((rows, q_width), BF16),) + (shape((BLOCK, half), BF16),) * (rows // BLOCK),
        in_specs=[SMEM, SMEM] + [VMEM] * (1 + len(got) + 2 * kv_heads + 3),
        out_specs=(VMEM,) * (1 + rows // BLOCK),
        compiler_params=params(16),
        name="norm",
    )(core, place, held, *got, *queries, *intras, col, gain, out_weight)
    received = [swap_head(part) for part in theirs]
    mine = pl.pallas_call(
        own_kernel,
        out_shape=shape((rows, half), F32),
        in_specs=[SMEM, VMEM, VMEM],
        out_specs=VMEM,
        compiler_params=params(16),
        name="own",
    )(core, normed, out_weight)
    out = ()
    for part in range(rows // BLOCK):
        out = (
            pl.pallas_call(
                add_kernel,
                grid=(ADD_STEPS,),
                out_shape=shape((rows, half), BF16),
                in_specs=[VMEM, VMEM] + [HBM] * len(out),
                out_specs=pl.BlockSpec(
                    (BLOCK // ADD_STEPS, half), lambda i, part=part: (i + part * ADD_STEPS, 0)
                ),
                input_output_aliases={2: 0} if out else {},
                compiler_params=params(8),
                name=f"add_{part}",
            )(mine, received[part], *out),
        )
    return out[0]


def solution(mesh):
    return jax.shard_map(
        on_device,
        mesh=mesh,
        in_specs=(
            P("seq", "head"),
            P(None, "head"),
            P(None, "head"),
            P(None, "head"),
            P("head"),
            P("head", None),
            P("seq"),
        ),
        out_specs=P("seq", "head"),
        check_vma=False,
    )
```

```python
import jax
import jax.numpy as jnp
from jax import lax
from jax.experimental import pallas as pl
from jax.experimental.pallas import tpu as pltpu
from jax.sharding import PartitionSpec as P

HEAD = 128
ID_ROWS = 8
BLOCK = 256
NORM_BLOCK = 512
ROUNDS = ((1, 2, 3), (6,), (8, 24, 16), (32, 96, 64))
INTRA_STEPS = (2, 3)
CHUNKS = 2
STAGE_COPIES = 4
ADD_STEPS = 2
EPSILON = 1e-05
F32 = jnp.float32
BF16 = jnp.bfloat16

SMEM = pl.BlockSpec(memory_space=pltpu.SMEM)
VMEM = pl.BlockSpec(memory_space=pltpu.VMEM)
HBM = pl.BlockSpec(memory_space=pltpu.HBM)


def params(mib):
    return pltpu.CompilerParams(vmem_limit_bytes=mib << 20)


def dot(a, b):
    return jnp.dot(a, b, preferred_element_type=F32)


def features(x):
    return jnp.where(x > 0.0, x + 1.0, jnp.exp(jnp.minimum(x, 0.0)))


def project(core_ref, own_ref, other_ref, weight_ref):
    half = own_ref.shape[1]
    mine = pl.multiple_of(core_ref[0] * half, half)
    theirs = pl.multiple_of((1 - core_ref[0]) * half, half)
    return dot(own_ref[...], weight_ref[pl.ds(mine, half), :]) + dot(
        other_ref[...], weight_ref[pl.ds(theirs, half), :]
    )


def own_half_kernel(core_ref, ids_hbm, own_hbm, wk_hbm, wv_hbm, *refs):
    own_ref, wk_ref, wv_ref, k_ref, v_ref, col_ref, row_ref, ids_vmem, sems = refs
    half = own_hbm.shape[1]
    chunk = half // CHUNKS
    near = core_ref[0] * half
    far = pl.multiple_of((1 - core_ref[0]) * half, half)
    copies = []
    for c in range(CHUNKS):
        cut = pl.ds(pl.multiple_of(near + c * chunk, chunk), chunk)
        copies.append((own_hbm.at[:, c * chunk : (c + 1) * chunk], own_ref.at[:, c * chunk : (c + 1) * chunk]))
        copies.append((wk_hbm.at[cut, :], wk_ref.at[cut, :]))
        copies.append((wv_hbm.at[cut, :], wv_ref.at[cut, :]))
    cut = pl.ds(far, half)
    copies.append((wk_hbm.at[cut, :], wk_ref.at[cut, :]))
    copies.append((wv_hbm.at[cut, :], wv_ref.at[cut, :]))
    copies.insert(0, (ids_hbm, ids_vmem))
    copies = [pltpu.make_async_copy(a, b, sems.at[i]) for i, (a, b) in enumerate(copies)]
    for copy in copies:
        copy.start()
    copies[0].wait()
    ids = ids_vmem[...].astype(F32)
    row_ref[...] = jnp.broadcast_to(ids, row_ref.shape)
    col_ref[...] = jnp.broadcast_to(ids, (HEAD, ids.shape[1])).T
    for c in range(CHUNKS):
        for copy in copies[3 * c + 1 : 3 * c + 4]:
            copy.wait()
        own = own_ref[:, c * chunk : (c + 1) * chunk]
        cut = pl.ds(pl.multiple_of(near + c * chunk, chunk), chunk)
        key = dot(own, wk_ref[cut, :])
        value = dot(own, wv_ref[cut, :])
        if c == 0:
            k_ref[...] = key
            v_ref[...] = value
        else:
            k_ref[...] += key
            v_ref[...] += value
    for copy in copies[3 * CHUNKS + 1 :]:
        copy.wait()


def key_value_kernel(core_ref, other_ref, k_part_ref, v_part_ref, wk_ref, wv_ref, col_ref, *outs):
    k_ref, v_ref, message_ref = outs
    rows, half = other_ref.shape
    other = other_ref[...]
    far = pl.ds(pl.multiple_of((1 - core_ref[0]) * half, half), half)
    key = features(k_part_ref[...] + dot(other, wk_ref[far, :])).astype(BF16)
    value = (v_part_ref[...] + dot(other, wv_ref[far, :])).astype(BF16)
    k_ref[...] = key
    v_ref[...] = value
    last = col_ref[rows - 1 : rows, :]
    tail = col_ref[...] == last
    heads = key.shape[1] // HEAD
    for h in range(heads):
        cut = slice(h * HEAD, (h + 1) * HEAD)
        tail_key = jnp.where(tail, key[:, cut].astype(F32), 0.0).astype(BF16)
        state = lax.dot_general(
            tail_key, value[:, cut], (((0,), (0,)), ((), ())), preferred_element_type=F32
        )
        message_ref[cut, :] = state.astype(BF16)
    message_ref[heads * HEAD :, :] = jnp.broadcast_to(last, (ID_ROWS, HEAD)).astype(BF16)


def stage_kernel(after_ref, weight_hbm, weight_ref, sems):
    size = weight_ref.shape[0] // STAGE_COPIES
    copies = []
    for i in range(STAGE_COPIES):
        cut = slice(i * size, (i + 1) * size)
        copies.append(pltpu.make_async_copy(weight_hbm.at[cut, :], weight_ref.at[cut, :], sems.at[i]))
    for copy in copies:
        copy.start()
    for copy in copies:
        copy.wait()


def intra_kernel(core_ref, own_ref, other_ref, wq_ref, k_ref, v_ref, col_ref, row_ref, q_ref, intra_ref):
    rows = own_ref.shape[0]
    group = wq_ref.shape[1] // HEAD
    q_ref[...] = features(project(core_ref, own_ref, other_ref, wq_ref)).astype(BF16)
    for start in range(0, rows, BLOCK):
        seen = start + BLOCK
        here = slice(start, seen)
        key = k_ref[:seen, :]
        value = v_ref[:seen, :]
        t = lax.broadcasted_iota(jnp.int32, (BLOCK, seen), 0) + start
        s = lax.broadcasted_iota(jnp.int32, (BLOCK, seen), 1)
        same = (col_ref[here, :1] == row_ref[:1, :seen]) & (t >= s)
        for g in range(group):
            cut = slice(g * HEAD, (g + 1) * HEAD)
            scores = lax.dot_general(
                q_ref[here, cut], key, (((1,), (1,)), ((), ())), preferred_element_type=F32
            )
            scores = jnp.where(same, scores, 0.0).astype(BF16)
            intra_ref[here, cut] = dot(scores, value)


def combine_kernel(bits, has_held, place_ref, col_ref, message_ref, *refs):
    got = refs[: len(bits)]
    held_in = refs[len(bits)] if has_held else None
    next_ref, held_ref = refs[-2:]
    rows = message_ref.shape[0] - ID_ROWS
    own_id = message_ref[rows : rows + 1, :].astype(F32)
    ids = [g[rows : rows + 1, :].astype(F32) for g in got]
    top = own_id
    for i in ids:
        top = jnp.maximum(top, i)
    first = col_ref[:1, :]
    total = jnp.where(own_id == top, message_ref[:rows, :].astype(F32), 0.0)
    held = held_in[...] if has_held else jnp.zeros((rows, HEAD), F32)
    for b, g, i in zip(bits, got, ids):
        state = g[:rows, :].astype(F32)
        earlier = (place_ref[0] & (1 << (b.bit_length() - 1))) != 0
        held = held + jnp.where((i == first) & earlier, state, 0.0)
        total = total + jnp.where(i == top, state, 0.0)
    next_ref[:rows, :] = total.astype(BF16)
    next_ref[rows:, :] = jnp.broadcast_to(top, (ID_ROWS, HEAD)).astype(BF16)
    held_ref[...] = held


def incoming_of(bits, place_ref, col_ref, held_ref, got):
    first = col_ref[:1, :]
    rows = held_ref.shape[0]
    held = held_ref[...]
    for b, g in zip(bits, got):
        earlier = (place_ref[0] & (1 << (b.bit_length() - 1))) != 0
        same = (g[rows : rows + 1, :].astype(F32) == first) & earlier
        held = held + jnp.where(same, g[:rows, :].astype(F32), 0.0)
    return held.astype(BF16)


def norm_kernel(bits, groups, core_ref, place_ref, held_ref, *refs):
    got, refs = refs[: len(bits)], refs[len(bits) :]
    queries, intras, refs = refs[:groups], refs[groups : 2 * groups], refs[2 * groups :]
    col_ref, gain_ref, weight_ref, normed_ref, *theirs = refs
    incoming = incoming_of(bits, place_ref, col_ref, held_ref, got)
    for start in range(0, col_ref.shape[0], NORM_BLOCK):
        here = slice(start, start + NORM_BLOCK)
        joins = col_ref[here, :] == col_ref[:1, :]
        for k in range(groups):
            width = queries[k].shape[1]
            for g in range(width // HEAD):
                cut = slice(g * HEAD, (g + 1) * HEAD)
                out = slice(k * width + g * HEAD, k * width + (g + 1) * HEAD)
                carried = dot(queries[k][here, cut], incoming[k * HEAD : (k + 1) * HEAD, :])
                combined = intras[k][here, cut] + jnp.where(joins, carried, 0.0)
                scale = lax.rsqrt(jnp.mean(combined * combined, axis=-1, keepdims=True) + EPSILON)
                normed_ref[here, out] = (combined * scale * gain_ref[:1, out]).astype(BF16)
    product = dot(normed_ref[...], columns(weight_ref, 1 - core_ref[0])).astype(BF16)
    size = theirs[0].shape[0]
    for i, part in enumerate(theirs):
        part[...] = product[i * size : (i + 1) * size, :]


def columns(weight_ref, part):
    half = weight_ref.shape[1] // 2
    return weight_ref[:, pl.ds(pl.multiple_of(part * half, half), half)]


def own_kernel(core_ref, normed_ref, weight_ref, out_ref):
    out_ref[...] = dot(normed_ref[...], columns(weight_ref, core_ref[0]))


def add_kernel(mine_ref, theirs_ref, *refs):
    out_ref = refs[-1]
    size = out_ref.shape[0]
    step = pl.program_id(0)
    first = pl.multiple_of((step + (pl.num_programs(0) if len(refs) > 1 else 0)) * size, size)
    here = pl.ds(pl.multiple_of(step * size, size), size)
    out_ref[...] = (mine_ref[pl.ds(first, size), :] + theirs_ref[here, :].astype(F32)).astype(BF16)


def shape(dims, dtype):
    return jax.ShapeDtypeStruct(dims, dtype)


def in_hbm(x):
    return pltpu.with_memory_space_constraint(x, pltpu.HBM)


def swap_head(x):
    return lax.ppermute(x, "head", [(0, 1), (1, 0)])


def on_device(tokens, q_weight, key_matrix, value_matrix, norm_gain, out_weight, doc_ids):
    rows, half = tokens.shape
    kv_width = key_matrix.shape[1]
    q_width = q_weight.shape[1]
    kv_heads = kv_width // HEAD
    group_width = q_width // kv_heads
    state_rows = kv_heads * HEAD
    count = lax.axis_size("seq")
    core = lax.axis_index("head").astype(jnp.int32).reshape(1)
    place = lax.axis_index("seq").astype(jnp.int32).reshape(1)
    other = swap_head(tokens)
    gain = norm_gain.reshape(1, q_width)
    own, wk, wv, k_part, v_part, col, row = pl.pallas_call(
        own_half_kernel,
        out_shape=(
            shape(tokens.shape, BF16),
            shape(key_matrix.shape, BF16),
            shape(value_matrix.shape, BF16),
            shape((rows, kv_width), F32),
            shape((rows, kv_width), F32),
            shape((rows, HEAD), F32),
            shape((8, rows), F32),
        ),
        in_specs=[SMEM, HBM, HBM, HBM, HBM],
        out_specs=(VMEM,) * 7,
        scratch_shapes=[pltpu.VMEM((1, rows), jnp.int32), pltpu.SemaphoreType.DMA((3 * CHUNKS + 3,))],
        compiler_params=params(8),
        name="own_half",
    )(core, *(in_hbm(x) for x in (doc_ids.reshape(1, rows), tokens, key_matrix, value_matrix)))

    key, value, message = pl.pallas_call(
        key_value_kernel,
        out_shape=(
            shape((rows, kv_width), BF16),
            shape((rows, kv_width), BF16),
            shape((state_rows + ID_ROWS, HEAD), BF16),
        ),
        in_specs=[SMEM] + [VMEM] * 6,
        out_specs=(VMEM, VMEM, VMEM),
        compiler_params=params(16),
        name="key_value",
    )(core, other, k_part, v_part, wk, wv, col)

    def intra(k, key, value):
        return pl.pallas_call(
            intra_kernel,
            out_shape=(shape((rows, group_width), BF16), shape((rows, group_width), F32)),
            grid=(1,),
            in_specs=[
                SMEM,
                VMEM,
                VMEM,
                pl.BlockSpec((2 * half, group_width), lambda i: (0, k)),
                pl.BlockSpec((rows, HEAD), lambda i: (0, k)),
                pl.BlockSpec((rows, HEAD), lambda i: (0, k)),
                VMEM,
                VMEM,
            ],
            out_specs=(VMEM, VMEM),
            compiler_params=params(24),
            name=f"intra_{k}",
        )(core, own, other, wq, key, value, col, row)

    held = None
    queries, intras = [], []
    for step, bits in enumerate(ROUNDS):
        final = step == len(ROUNDS) - 1
        got = [lax.ppermute(message, "seq", [(i, i ^ b) for i in range(count)]) for b in bits]
        if step == 0:
            wq = pl.pallas_call(
                stage_kernel,
                out_shape=shape(q_weight.shape, BF16),
                in_specs=[VMEM, HBM],
                out_specs=VMEM,
                scratch_shapes=[pltpu.SemaphoreType.DMA((STAGE_COPIES,))],
                compiler_params=params(2),
                name="stage",
            )(message, in_hbm(q_weight))
        if step in INTRA_STEPS:
            (key, value), _ = lax.optimization_barrier(((key, value), message))
            query, part = intra(INTRA_STEPS.index(step), key, value)
            queries.append(query)
            intras.append(part)
        if final:
            break
        extra = () if held is None else (held,)
        message, held = pl.pallas_call(
            lambda *refs, bits=bits, has=held is not None: combine_kernel(bits, has, *refs),
            out_shape=(shape(message.shape, BF16), shape((state_rows, HEAD), F32)),
            in_specs=[SMEM] + [VMEM] * (2 + len(bits) + len(extra)),
            out_specs=(VMEM, VMEM),
            compiler_params=params(4),
            name="combine",
        )(place, col, message, *got, *extra)
        if step == 0:
            message, wq = lax.optimization_barrier((message, wq))
        if step in INTRA_STEPS and not final:
            message, queries[-1] = lax.optimization_barrier((message, queries[-1]))

    normed, *theirs = pl.pallas_call(
        lambda *refs: norm_kernel(ROUNDS[-1], kv_heads, *refs),
        out_shape=(shape((rows, q_width), BF16),) + (shape((BLOCK, half), BF16),) * (rows // BLOCK),
        in_specs=[SMEM, SMEM] + [VMEM] * (1 + len(got) + 2 * kv_heads + 3),
        out_specs=(VMEM,) * (1 + rows // BLOCK),
        compiler_params=params(16),
        name="norm",
    )(core, place, held, *got, *queries, *intras, col, gain, out_weight)
    received = [swap_head(part) for part in theirs]
    mine = pl.pallas_call(
        own_kernel,
        out_shape=shape((rows, half), F32),
        in_specs=[SMEM, VMEM, VMEM],
        out_specs=VMEM,
        compiler_params=params(16),
        name="own",
    )(core, normed, out_weight)
    out = ()
    for part in range(rows // BLOCK):
        out = (
            pl.pallas_call(
                add_kernel,
                grid=(ADD_STEPS,),
                out_shape=shape((rows, half), BF16),
                in_specs=[VMEM, VMEM] + [HBM] * len(out),
                out_specs=pl.BlockSpec(
                    (BLOCK // ADD_STEPS, half), lambda i, part=part: (i + part * ADD_STEPS, 0)
                ),
                input_output_aliases={2: 0} if out else {},
                compiler_params=params(8),
                name=f"add_{part}",
            )(mine, received[part], *out),
        )
    return out[0]


def solution(mesh):
    return jax.shard_map(
        on_device,
        mesh=mesh,
        in_specs=(
            P("seq", "head"),
            P(None, "head"),
            P(None, "head"),
            P(None, "head"),
            P("head"),
            P("head", None),
            P("seq"),
        ),
        out_specs=P("seq", "head"),
        check_vma=False,
    )
```

```python
import jax
import jax.numpy as jnp
from jax import lax
from jax.experimental import pallas as pl
from jax.experimental.pallas import tpu as pltpu
from jax.sharding import PartitionSpec as P

HEAD = 128
ID_ROWS = 8
BLOCK = 256
NORM_BLOCK = 512
ROUNDS = ((1, 2, 3), (6,), (8, 24, 16), (32, 96, 64))
INTRA_STEPS = (2, 3)
CHUNKS = 2
STAGE_COPIES = 4
ADD_STEPS = 1
EPSILON = 1e-05
F32 = jnp.float32
BF16 = jnp.bfloat16

SMEM = pl.BlockSpec(memory_space=pltpu.SMEM)
VMEM = pl.BlockSpec(memory_space=pltpu.VMEM)
HBM = pl.BlockSpec(memory_space=pltpu.HBM)


def params(mib):
    return pltpu.CompilerParams(vmem_limit_bytes=mib << 20)


def dot(a, b):
    return jnp.dot(a, b, preferred_element_type=F32)


def features(x):
    return jnp.where(x > 0.0, x + 1.0, jnp.exp(jnp.minimum(x, 0.0)))


def project(core_ref, own_ref, other_ref, weight_ref):
    half = own_ref.shape[1]
    mine = pl.multiple_of(core_ref[0] * half, half)
    theirs = pl.multiple_of((1 - core_ref[0]) * half, half)
    return dot(own_ref[...], weight_ref[pl.ds(mine, half), :]) + dot(
        other_ref[...], weight_ref[pl.ds(theirs, half), :]
    )


def own_half_kernel(core_ref, ids_hbm, own_hbm, wk_hbm, wv_hbm, *refs):
    own_ref, wk_ref, wv_ref, k_ref, v_ref, col_ref, row_ref, ids_vmem, sems = refs
    half = own_hbm.shape[1]
    chunk = half // CHUNKS
    near = core_ref[0] * half
    far = pl.multiple_of((1 - core_ref[0]) * half, half)
    copies = []
    for c in range(CHUNKS):
        cut = pl.ds(pl.multiple_of(near + c * chunk, chunk), chunk)
        copies.append((own_hbm.at[:, c * chunk : (c + 1) * chunk], own_ref.at[:, c * chunk : (c + 1) * chunk]))
        copies.append((wk_hbm.at[cut, :], wk_ref.at[cut, :]))
        copies.append((wv_hbm.at[cut, :], wv_ref.at[cut, :]))
    cut = pl.ds(far, half)
    copies.append((wk_hbm.at[cut, :], wk_ref.at[cut, :]))
    copies.append((wv_hbm.at[cut, :], wv_ref.at[cut, :]))
    copies.insert(0, (ids_hbm, ids_vmem))
    copies = [pltpu.make_async_copy(a, b, sems.at[i]) for i, (a, b) in enumerate(copies)]
    for copy in copies:
        copy.start()
    copies[0].wait()
    ids = ids_vmem[...].astype(F32)
    row_ref[...] = jnp.broadcast_to(ids, row_ref.shape)
    col_ref[...] = jnp.broadcast_to(ids, (HEAD, ids.shape[1])).T
    for c in range(CHUNKS):
        for copy in copies[3 * c + 1 : 3 * c + 4]:
            copy.wait()
        own = own_ref[:, c * chunk : (c + 1) * chunk]
        cut = pl.ds(pl.multiple_of(near + c * chunk, chunk), chunk)
        key = dot(own, wk_ref[cut, :])
        value = dot(own, wv_ref[cut, :])
        if c == 0:
            k_ref[...] = key
            v_ref[...] = value
        else:
            k_ref[...] += key
            v_ref[...] += value
    for copy in copies[3 * CHUNKS + 1 :]:
        copy.wait()


def key_value_kernel(core_ref, other_ref, k_part_ref, v_part_ref, wk_ref, wv_ref, col_ref, *outs):
    k_ref, v_ref, message_ref = outs
    rows, half = other_ref.shape
    other = other_ref[...]
    far = pl.ds(pl.multiple_of((1 - core_ref[0]) * half, half), half)
    key = features(k_part_ref[...] + dot(other, wk_ref[far, :])).astype(BF16)
    value = (v_part_ref[...] + dot(other, wv_ref[far, :])).astype(BF16)
    k_ref[...] = key
    v_ref[...] = value
    last = col_ref[rows - 1 : rows, :]
    tail = col_ref[...] == last
    heads = key.shape[1] // HEAD
    tail_key = jnp.where(jnp.concatenate([tail] * heads, axis=1), key.astype(F32), 0.0).astype(BF16)
    state = lax.dot_general(tail_key, value, (((0,), (0,)), ((), ())), preferred_element_type=F32)
    for h in range(heads):
        cut = slice(h * HEAD, (h + 1) * HEAD)
        message_ref[cut, :] = state[cut, cut].astype(BF16)
    message_ref[heads * HEAD :, :] = jnp.broadcast_to(last, (ID_ROWS, HEAD)).astype(BF16)


def stage_kernel(after_ref, weight_hbm, weight_ref, sems):
    size = weight_ref.shape[0] // STAGE_COPIES
    copies = []
    for i in range(STAGE_COPIES):
        cut = slice(i * size, (i + 1) * size)
        copies.append(pltpu.make_async_copy(weight_hbm.at[cut, :], weight_ref.at[cut, :], sems.at[i]))
    for copy in copies:
        copy.start()
    for copy in copies:
        copy.wait()


def intra_kernel(core_ref, own_ref, other_ref, wq_ref, k_ref, v_ref, col_ref, row_ref, q_ref, intra_ref):
    rows = own_ref.shape[0]
    group = wq_ref.shape[1] // HEAD
    q_ref[...] = features(project(core_ref, own_ref, other_ref, wq_ref)).astype(BF16)
    for start in range(0, rows, BLOCK):
        seen = start + BLOCK
        here = slice(start, seen)
        key = k_ref[:seen, :]
        value = v_ref[:seen, :]
        t = lax.broadcasted_iota(jnp.int32, (BLOCK, seen), 0) + start
        s = lax.broadcasted_iota(jnp.int32, (BLOCK, seen), 1)
        same = (col_ref[here, :1] == row_ref[:1, :seen]) & (t >= s)
        for g in range(group):
            cut = slice(g * HEAD, (g + 1) * HEAD)
            scores = lax.dot_general(
                q_ref[here, cut], key, (((1,), (1,)), ((), ())), preferred_element_type=F32
            )
            scores = jnp.where(same, scores, 0.0).astype(BF16)
            intra_ref[here, cut] = dot(scores, value)


def combine_kernel(bits, has_held, place_ref, col_ref, message_ref, *refs):
    got = refs[: len(bits)]
    held_in = refs[len(bits)] if has_held else None
    next_ref, held_ref = refs[-2:]
    rows = message_ref.shape[0] - ID_ROWS
    own_id = message_ref[rows : rows + 1, :].astype(F32)
    ids = [g[rows : rows + 1, :].astype(F32) for g in got]
    top = own_id
    for i in ids:
        top = jnp.maximum(top, i)
    first = col_ref[:1, :]
    total = jnp.where(own_id == top, message_ref[:rows, :].astype(F32), 0.0)
    held = held_in[...] if has_held else jnp.zeros((rows, HEAD), F32)
    for b, g, i in zip(bits, got, ids):
        state = g[:rows, :].astype(F32)
        earlier = (place_ref[0] & (1 << (b.bit_length() - 1))) != 0
        held = held + jnp.where((i == first) & earlier, state, 0.0)
        total = total + jnp.where(i == top, state, 0.0)
    next_ref[:rows, :] = total.astype(BF16)
    next_ref[rows:, :] = jnp.broadcast_to(top, (ID_ROWS, HEAD)).astype(BF16)
    held_ref[...] = held


def incoming_of(bits, place_ref, col_ref, held_ref, got):
    first = col_ref[:1, :]
    rows = held_ref.shape[0]
    held = held_ref[...]
    for b, g in zip(bits, got):
        earlier = (place_ref[0] & (1 << (b.bit_length() - 1))) != 0
        same = (g[rows : rows + 1, :].astype(F32) == first) & earlier
        held = held + jnp.where(same, g[:rows, :].astype(F32), 0.0)
    return held.astype(BF16)


def norm_kernel(bits, groups, core_ref, place_ref, held_ref, *refs):
    got, refs = refs[: len(bits)], refs[len(bits) :]
    queries, intras, refs = refs[:groups], refs[groups : 2 * groups], refs[2 * groups :]
    col_ref, gain_ref, weight_ref, normed_ref, *theirs = refs
    incoming = incoming_of(bits, place_ref, col_ref, held_ref, got)
    for start in range(0, col_ref.shape[0], NORM_BLOCK):
        here = slice(start, start + NORM_BLOCK)
        joins = col_ref[here, :] == col_ref[:1, :]
        for k in range(groups):
            width = queries[k].shape[1]
            for g in range(width // HEAD):
                cut = slice(g * HEAD, (g + 1) * HEAD)
                out = slice(k * width + g * HEAD, k * width + (g + 1) * HEAD)
                carried = dot(queries[k][here, cut], incoming[k * HEAD : (k + 1) * HEAD, :])
                combined = intras[k][here, cut] + jnp.where(joins, carried, 0.0)
                scale = lax.rsqrt(jnp.mean(combined * combined, axis=-1, keepdims=True) + EPSILON)
                normed_ref[here, out] = (combined * scale * gain_ref[:1, out]).astype(BF16)
    product = dot(normed_ref[...], columns(weight_ref, 1 - core_ref[0])).astype(BF16)
    size = theirs[0].shape[0]
    for i, part in enumerate(theirs):
        part[...] = product[i * size : (i + 1) * size, :]


def columns(weight_ref, part):
    half = weight_ref.shape[1] // 2
    return weight_ref[:, pl.ds(pl.multiple_of(part * half, half), half)]


def own_kernel(core_ref, normed_ref, weight_ref, out_ref):
    out_ref[...] = dot(normed_ref[...], columns(weight_ref, core_ref[0]))


def add_kernel(mine_ref, theirs_ref, *refs):
    out_ref = refs[-1]
    size = out_ref.shape[0]
    step = pl.program_id(0)
    first = pl.multiple_of((step + (pl.num_programs(0) if len(refs) > 1 else 0)) * size, size)
    here = pl.ds(pl.multiple_of(step * size, size), size)
    out_ref[...] = (mine_ref[pl.ds(first, size), :] + theirs_ref[here, :].astype(F32)).astype(BF16)


def shape(dims, dtype):
    return jax.ShapeDtypeStruct(dims, dtype)


def in_hbm(x):
    return pltpu.with_memory_space_constraint(x, pltpu.HBM)


def swap_head(x):
    return lax.ppermute(x, "head", [(0, 1), (1, 0)])


def on_device(tokens, q_weight, key_matrix, value_matrix, norm_gain, out_weight, doc_ids):
    rows, half = tokens.shape
    kv_width = key_matrix.shape[1]
    q_width = q_weight.shape[1]
    kv_heads = kv_width // HEAD
    group_width = q_width // kv_heads
    state_rows = kv_heads * HEAD
    count = lax.axis_size("seq")
    core = lax.axis_index("head").astype(jnp.int32).reshape(1)
    place = lax.axis_index("seq").astype(jnp.int32).reshape(1)
    other = swap_head(tokens)
    gain = norm_gain.reshape(1, q_width)
    own, wk, wv, k_part, v_part, col, row = pl.pallas_call(
        own_half_kernel,
        out_shape=(
            shape(tokens.shape, BF16),
            shape(key_matrix.shape, BF16),
            shape(value_matrix.shape, BF16),
            shape((rows, kv_width), F32),
            shape((rows, kv_width), F32),
            shape((rows, HEAD), F32),
            shape((8, rows), F32),
        ),
        in_specs=[SMEM, HBM, HBM, HBM, HBM],
        out_specs=(VMEM,) * 7,
        scratch_shapes=[pltpu.VMEM((1, rows), jnp.int32), pltpu.SemaphoreType.DMA((3 * CHUNKS + 3,))],
        compiler_params=params(8),
        name="own_half",
    )(core, *(in_hbm(x) for x in (doc_ids.reshape(1, rows), tokens, key_matrix, value_matrix)))

    key, value, message = pl.pallas_call(
        key_value_kernel,
        out_shape=(
            shape((rows, kv_width), BF16),
            shape((rows, kv_width), BF16),
            shape((state_rows + ID_ROWS, HEAD), BF16),
        ),
        in_specs=[SMEM] + [VMEM] * 6,
        out_specs=(VMEM, VMEM, VMEM),
        compiler_params=params(16),
        name="key_value",
    )(core, other, k_part, v_part, wk, wv, col)

    def intra(k, key, value):
        return pl.pallas_call(
            intra_kernel,
            out_shape=(shape((rows, group_width), BF16), shape((rows, group_width), F32)),
            grid=(1,),
            in_specs=[
                SMEM,
                VMEM,
                VMEM,
                pl.BlockSpec((2 * half, group_width), lambda i: (0, k)),
                pl.BlockSpec((rows, HEAD), lambda i: (0, k)),
                pl.BlockSpec((rows, HEAD), lambda i: (0, k)),
                VMEM,
                VMEM,
            ],
            out_specs=(VMEM, VMEM),
            compiler_params=params(24),
            name=f"intra_{k}",
        )(core, own, other, wq, key, value, col, row)

    held = None
    queries, intras = [], []
    for step, bits in enumerate(ROUNDS):
        final = step == len(ROUNDS) - 1
        got = [lax.ppermute(message, "seq", [(i, i ^ b) for i in range(count)]) for b in bits]
        if step == 0:
            wq = pl.pallas_call(
                stage_kernel,
                out_shape=shape(q_weight.shape, BF16),
                in_specs=[VMEM, HBM],
                out_specs=VMEM,
                scratch_shapes=[pltpu.SemaphoreType.DMA((STAGE_COPIES,))],
                compiler_params=params(2),
                name="stage",
            )(message, in_hbm(q_weight))
        if step in INTRA_STEPS:
            (key, value), _ = lax.optimization_barrier(((key, value), message))
            query, part = intra(INTRA_STEPS.index(step), key, value)
            queries.append(query)
            intras.append(part)
        if final:
            break
        extra = () if held is None else (held,)
        message, held = pl.pallas_call(
            lambda *refs, bits=bits, has=held is not None: combine_kernel(bits, has, *refs),
            out_shape=(shape(message.shape, BF16), shape((state_rows, HEAD), F32)),
            in_specs=[SMEM] + [VMEM] * (2 + len(bits) + len(extra)),
            out_specs=(VMEM, VMEM),
            compiler_params=params(4),
            name="combine",
        )(place, col, message, *got, *extra)
        if step == 0:
            message, wq = lax.optimization_barrier((message, wq))
        if step in INTRA_STEPS and not final:
            message, queries[-1] = lax.optimization_barrier((message, queries[-1]))

    normed, *theirs = pl.pallas_call(
        lambda *refs: norm_kernel(ROUNDS[-1], kv_heads, *refs),
        out_shape=(shape((rows, q_width), BF16),) + (shape((BLOCK, half), BF16),) * (rows // BLOCK),
        in_specs=[SMEM, SMEM] + [VMEM] * (1 + len(got) + 2 * kv_heads + 3),
        out_specs=(VMEM,) * (1 + rows // BLOCK),
        compiler_params=params(16),
        name="norm",
    )(core, place, held, *got, *queries, *intras, col, gain, out_weight)
    received = [swap_head(part) for part in theirs]
    mine = pl.pallas_call(
        own_kernel,
        out_shape=shape((rows, half), F32),
        in_specs=[SMEM, VMEM, VMEM],
        out_specs=VMEM,
        compiler_params=params(16),
        name="own",
    )(core, normed, out_weight)
    out = ()
    for part in range(rows // BLOCK):
        out = (
            pl.pallas_call(
                add_kernel,
                grid=(ADD_STEPS,),
                out_shape=shape((rows, half), BF16),
                in_specs=[VMEM, VMEM] + [HBM] * len(out),
                out_specs=pl.BlockSpec(
                    (BLOCK // ADD_STEPS, half), lambda i, part=part: (i + part * ADD_STEPS, 0)
                ),
                input_output_aliases={2: 0} if out else {},
                compiler_params=params(8),
                name=f"add_{part}",
            )(mine, received[part], *out),
        )
    return out[0]


def solution(mesh):
    return jax.shard_map(
        on_device,
        mesh=mesh,
        in_specs=(
            P("seq", "head"),
            P(None, "head"),
            P(None, "head"),
            P(None, "head"),
            P("head"),
            P("head", None),
            P("seq"),
        ),
        out_specs=P("seq", "head"),
        check_vma=False,
    )
```
